128 devices in a mesh: ep: 128 (over z, x, y, core).
Axes of the slice: x: 4, y: 4, z: 4, core: 2. Of those that a mesh axis runs over, the one named last changes fastest.
Arguments:
- tokens: bfloat16 [2, 2048, 3584], P(None, 'ep'), may hold values from -6 to 6
- expert_ids: int32 [2, 2048, 8], P(None, 'ep'), may hold values from 0 to 127, all different within a row; in each aligned block of 16 rows (0 to 15, 16 to 31, ..., all dimensions but the last counted through in order) at most 2 rows name the same one
- combine_weights: float32 [2, 2048, 8], P(None, 'ep'), may hold values from 0.05 to 0.5
- w_gate: bfloat16 [128, 3584, 1024], P('ep'), may hold values from -0.09375 to 0.09375
- w_up: bfloat16 [128, 3584, 1024], P('ep'), may hold values from -0.09375 to 0.09375
- w_down: bfloat16 [128, 1024, 3584], P('ep'), may hold values from -0.1875 to 0.1875
- shared_weights: bfloat16 [3, 3584, 16384], P(None, None, 'ep'), as said below
Outputs:
- moe_out: bfloat16 [2, 2048, 3584], P(None, 'ep')
The draws below stay inside these ranges and needn't reach their ends.
Inputs may be any that keep to these rules, and one draw needn't show every extreme that they name: `expert_ids`: in each step the 16 rows of one device name any one expert at most 2 times; the 8 experts of a token differ. `shared_weights`: the array is 16 equal copies of one block of 1024 columns, laid end to end along the last dimension.
All inputs are finite; a program needn't handle non-finite values.
Results may differ from the reference program's by a relative error of at most 0.0055.
Values may be sent and summed in bfloat16 or wider, within the bound.
A program may use at most 128 MiB of HBM per device.

```python
import math
import jax
import jax.numpy as jnp
import numpy as np
from jax import lax

D = 3584
FFE = 1024
FS = 1024
TOPK = 8
STEPS = 2
REQ_DEV = 16
TOKENS = 2048
EXPERTS = 128
CAP = 2
SHARED_COLS = 16384
N_EP = 128


def draw_shared_weights(key, part):
    scale = D ** (-0.5)
    block = jnp.clip(jax.random.normal(key, (3, D, FS), jnp.float32), -6.0, 6.0) * scale
    copies = SHARED_COLS // FS
    return jnp.tile(block, (1, 1, copies)).astype(jnp.bfloat16)


def block_scale(rng, shape, pieces, smallest, top_value):
    gain = 1.0
    for dim, shards_of in pieces:
        draws = jax.random.uniform(jax.random.fold_in(jax.random.fold_in(rng, 6), dim), (shards_of,), jnp.float32, smallest / len(pieces), top_value / len(pieces))
        gain = gain * jnp.repeat(jnp.exp(draws), shape[dim] // shards_of).reshape((-1,) + (1,) * (len(shape) - 1 - dim))
    return gain


def assign_block(key, own, number, rows, number_of, top, most, skew):
    order = jax.random.permutation(key, number_of)
    heavy_load, ordinary = shares(number_of, rows * top, most, skew, True), shares(number_of, rows * top, most, skew, False)
    places = jnp.arange(number_of)

    def named(lengths, offset_by):
        used = int((lengths > 0).sum())
        fixed = max(1, used // 4)
        moved = fixed + (places - fixed + offset_by * (used - fixed)) % max(1, number_of - fixed)
        return jnp.zeros((number_of,), jnp.int32).at[order[jnp.where(places < fixed, places, moved)]].set(jnp.asarray(lengths, jnp.int32))

    lengths = jnp.where(number % 4 == 0, named(heavy_load, number // 4), named(ordinary, number - number // 4 - 1))
    mixed = jax.random.permutation(jax.random.fold_in(own, 3), number_of)
    giver, sink = mixed[0:number_of // 2 * 2:2], mixed[1:number_of // 2 * 2:2]
    room = jnp.minimum(lengths[giver] - 1, most - lengths[sink]) // 2
    room = jnp.where((giver == order[0]) | (sink == order[0]) | (lengths[sink] == 0), 0, jnp.maximum(room, 0))
    moved = jax.random.randint(jax.random.fold_in(own, 4), (number_of // 2,), 0, 1 << 20) % (room + 1)
    lengths = lengths.at[giver].add(-moved).at[sink].add(moved)
    labels = jnp.searchsorted(jnp.cumsum(lengths), jnp.arange(rows * top), side="right").astype(jnp.int32)
    table = labels.reshape(top, rows).T
    table = table[jax.random.permutation(jax.random.fold_in(own, 1), rows)]
    offset_by = jax.random.randint(jax.random.fold_in(own, 2), (rows, 1), 0, top)
    return jnp.take_along_axis(table, (jnp.arange(top)[None, :] + offset_by) % top, axis=1)


def shares(amount, total, reach, slope, full):
    portions = [(1 << 20) // math.isqrt(rank ** slope) + 1 for rank in range(1, amount + 1)]
    largest = reach if full else min(reach, max(-(-total // amount), total * portions[0] // sum(portions)))
    least = 1 if total - largest >= amount - 1 else 0
    holding, spare = [largest] + [least] * (amount - 1), total - largest - least * (amount - 1)
    while spare > 0:
        movable = [i for i in range(1, amount) if holding[i] < largest] or [i for i in range(1, amount) if holding[i] < reach]
        mass, left = sum([portions[i] for i in movable]), spare
        for i in movable:
            extra = min(reach - holding[i], max(1, left * portions[i] // mass), spare)
            holding[i] = holding[i] + extra
            spare = spare - extra
    return np.array(holding)


def bell_draw(own_key, dims, scale, limit, pieces=(), kind=jnp.bfloat16):
    entries = jax.random.normal(own_key, dims, jnp.float32) * scale
    if len(pieces) > 0:
        entries = block_scale(own_key, dims, pieces, -0.22, 0.18) * entries
    return jnp.clip(entries, min=-limit, max=limit).astype(kind)


def setup_inputs(seed: int = 0) -> dict:
    arg_keys = jax.random.split(jax.random.key(seed), 8)
    tokens = bell_draw(arg_keys[0], (STEPS, TOKENS, D), 1.0, 6.0, ((1, 128),))
    expert_ids_keys = jax.random.split(jax.random.fold_in(arg_keys[1], 1), STEPS * TOKENS // REQ_DEV)
    expert_ids_turns = jax.random.permutation(jax.random.fold_in(arg_keys[1], 3), STEPS * TOKENS // REQ_DEV)
    expert_ids = jax.vmap(lambda own, number: assign_block(jax.random.fold_in(arg_keys[1], 2), own, number, REQ_DEV, EXPERTS, TOPK, CAP, 2))(expert_ids_keys, expert_ids_turns).reshape((STEPS, TOKENS, TOPK))
    combine_weights = jnp.clip(jnp.exp(math.log(0.5) - 2.3025851 * jax.random.uniform(arg_keys[2], (STEPS, TOKENS, TOPK), jnp.float32) ** block_scale(arg_keys[2], (STEPS, TOKENS, TOPK), ((1, 128),), -0.2, 0.2)), 0.05, 0.5)
    w_gate = bell_draw(arg_keys[3], (EXPERTS, D, FFE), D ** -0.5, 0.09375, ((0, 128),))
    w_up = bell_draw(arg_keys[4], (EXPERTS, D, FFE), D ** -0.5, 0.09375, ((0, 128),))
    w_down = bell_draw(arg_keys[5], (EXPERTS, FFE, D), FFE ** -0.5, 0.1875, ((0, 128),))
    shared_weights = draw_shared_weights(jax.random.fold_in(arg_keys[7], 71), 0)
    return {"tokens": tokens, "expert_ids": expert_ids, "combine_weights": combine_weights, "w_gate": w_gate, "w_up": w_up, "w_down": w_down, "shared_weights": shared_weights}


def expert_rows(token_rows, gate_mat, up_mat, down_mat):
    gate_val = jnp.dot(token_rows, gate_mat, preferred_element_type=jnp.float32)
    up_val = jnp.dot(token_rows, up_mat, preferred_element_type=jnp.float32)
    hidden = (jax.nn.silu(gate_val) * up_val).astype(jnp.bfloat16)
    return jnp.dot(hidden, down_mat, preferred_element_type=jnp.float32).astype(jnp.bfloat16)


def reference(tokens, expert_ids, combine_weights, w_gate, w_up, w_down, shared_weights):
    pairs = REQ_DEV * TOPK
    flat_ids = expert_ids.reshape(STEPS, N_EP, pairs)
    onehot = (flat_ids[..., None] == jnp.arange(EXPERTS, dtype=jnp.int32)).astype(jnp.int32)
    slot_index = jnp.sum((jnp.cumsum(onehot, axis=2) - onehot) * onehot, axis=3).astype(jnp.int32)
    local_tok = jnp.broadcast_to(jnp.arange(pairs, dtype=jnp.int32) // TOPK, (STEPS, N_EP, pairs))
    step_idx = jnp.broadcast_to(jnp.arange(STEPS, dtype=jnp.int32)[:, None, None], (STEPS, N_EP, pairs))
    block_idx = jnp.broadcast_to(jnp.arange(N_EP, dtype=jnp.int32)[None, :, None], (STEPS, N_EP, pairs))
    source = jnp.zeros((STEPS, N_EP, EXPERTS, CAP), jnp.int32).at[step_idx, block_idx, flat_ids, slot_index].set(local_tok)
    weight_tab = jnp.zeros((STEPS, N_EP, EXPERTS, CAP), jnp.float32).at[step_idx, block_idx, flat_ids, slot_index].set(
        combine_weights.reshape(STEPS, N_EP, pairs).astype(jnp.float32))
    grid = tokens.reshape(STEPS, N_EP, REQ_DEV, D)
    step_b = jnp.broadcast_to(jnp.arange(STEPS, dtype=jnp.int32)[:, None, None], (STEPS, N_EP, CAP))
    block_b = jnp.broadcast_to(jnp.arange(N_EP, dtype=jnp.int32)[None, :, None], (STEPS, N_EP, CAP))

    def one_expert(totals, inputs):
        gate_mat, up_mat, down_mat, src, wts = inputs
        chosen = jnp.take_along_axis(grid, src[..., None], axis=2)
        outputs = expert_rows(chosen.reshape(-1, D), gate_mat, up_mat, down_mat).reshape(STEPS, N_EP, CAP, D)
        weighted = outputs.astype(jnp.float32) * wts[..., None]
        return totals.at[step_b, block_b, src].add(weighted), None

    start = jnp.zeros((STEPS, N_EP, REQ_DEV, D), jnp.float32)
    routed, _ = lax.scan(one_expert, start, (w_gate, w_up, w_down,
                                             jnp.transpose(source, (2, 0, 1, 3)),
                                             jnp.transpose(weight_tab, (2, 0, 1, 3))))
    block_weights = shared_weights[:, :, :FS]
    flat_rows = tokens.reshape(-1, D)
    gate_val = jnp.dot(flat_rows, block_weights[0], preferred_element_type=jnp.float32)
    up_val = jnp.dot(flat_rows, block_weights[1], preferred_element_type=jnp.float32)
    shared_hidden = (jax.nn.silu(gate_val) * up_val).astype(jnp.bfloat16)
    shared_out = jnp.dot(shared_hidden, block_weights[2].T, preferred_element_type=jnp.float32)
    total = shared_out.reshape(STEPS, N_EP, REQ_DEV, D) + routed
    return total.reshape(STEPS, TOKENS, D).astype(jnp.bfloat16)
```

```python
import jax
import jax.numpy as jnp
from jax import lax
from jax.sharding import PartitionSpec as P


def partner_2(block, axis, apart):
    count = lax.axis_size(axis)
    route = []
    for low in range(count):
        high = low | 1 << apart
        if high != low and high < count:
            route += [(low, high), (high, low)]
    return lax.ppermute(block, axis, route)


def expert_rows(token_rows, gate_mat, up_mat, down_mat):
    gate_val = jnp.dot(token_rows, gate_mat, preferred_element_type=jnp.float32)
    up_val = jnp.dot(token_rows, up_mat, preferred_element_type=jnp.float32)
    hidden = (jax.nn.silu(gate_val) * up_val).astype(jnp.bfloat16)
    return jnp.dot(hidden, down_mat, preferred_element_type=jnp.float32).astype(jnp.bfloat16)


def route_tables(step_ids, step_weights, experts, capacity):
    row_count, top_count = step_ids.shape
    pair_count = row_count * top_count
    flat_ids = step_ids.reshape(pair_count)
    onehot = (flat_ids[:, None] == jnp.arange(experts, dtype=jnp.int32)[None, :]).astype(
        jnp.float32
    )
    earlier = (jnp.arange(pair_count)[:, None] > jnp.arange(pair_count)[None, :]).astype(
        jnp.float32
    )
    counts = jnp.dot(earlier, onehot, precision=lax.Precision.HIGHEST)
    slot_index = jnp.sum(counts * onehot, axis=1).astype(jnp.int32)
    position = flat_ids * capacity + slot_index
    placing = (
        position[:, None] == jnp.arange(experts * capacity, dtype=jnp.int32)[None, :]
    ).astype(jnp.float32)
    owner = (
        (jnp.arange(pair_count) // top_count)[:, None] == jnp.arange(row_count)[None, :]
    ).astype(jnp.float32)
    dispatch = jnp.dot(placing.T, owner, precision=lax.Precision.HIGHEST).astype(jnp.bfloat16)
    combine = jnp.dot(
        (owner * step_weights.reshape(pair_count)[:, None]).T,
        placing,
        precision=lax.Precision.HIGHEST,
    )
    return (dispatch, combine)


def join_halves(mine, partner, upper_side, axis_no):
    return jnp.where(
        upper_side,
        jnp.concatenate([partner, mine], axis=axis_no),
        jnp.concatenate([mine, partner], axis=axis_no),
    )


def shared_expert(tokens, shared_weights):
    my_index = lax.axis_index("ep")
    step_count, row_count, model_width = tokens.shape
    gathered = tokens
    for level in (2, 1, 0):
        partner = partner_2(gathered, "ep", level)
        gathered = join_halves(gathered, partner, my_index >> level & 1 == 1, 1)
    flat_rows = gathered.reshape(-1, model_width)
    gate_val = jnp.dot(flat_rows, shared_weights[0], preferred_element_type=jnp.float32)
    up_val = jnp.dot(flat_rows, shared_weights[1], preferred_element_type=jnp.float32)
    hidden = (jax.nn.silu(gate_val) * up_val).astype(jnp.bfloat16)
    partial_value = lax.dot_general(
        hidden, shared_weights[2], (((1,), (1,)), ((), ())), preferred_element_type=jnp.float32
    )
    partial_value = partial_value.reshape(step_count, 8 * row_count, model_width)
    for level in (0, 1, 2):
        half = partial_value.shape[1] // 2
        bit = my_index >> level & 1
        keep = lax.dynamic_slice_in_dim(partial_value, bit * half, half, 1)
        send = lax.dynamic_slice_in_dim(partial_value, (1 - bit) * half, half, 1)
        partial_value = keep + partner_2(send, "ep", level)
    return partial_value


def shards(tokens, expert_ids, combine_weights, w_gate, w_up, w_down, shared_weights):
    step_count, row_count, model_width = tokens.shape
    top_count = expert_ids.shape[2]
    device_count = lax.axis_size("ep")
    experts = w_gate.shape[0] * device_count
    capacity = max(2, row_count * top_count * 2 // experts)
    tables = [
        route_tables(expert_ids[s], combine_weights[s], experts, capacity)
        for s in range(step_count)
    ]
    outgoing = jnp.stack(
        [
            jnp.dot(tables[s][0], tokens[s], preferred_element_type=jnp.float32)
            .astype(jnp.bfloat16)
            .reshape(experts, capacity, model_width)
            for s in range(step_count)
        ]
    )
    received = lax.all_to_all(outgoing, "ep", split_axis=1, concat_axis=1, tiled=True)
    returned = lax.all_to_all(
        expert_rows(received.reshape(-1, model_width), w_gate[0], w_up[0], w_down[0]).reshape(
            received.shape
        ),
        "ep",
        split_axis=1,
        concat_axis=1,
        tiled=True,
    )
    shared = shared_expert(tokens, shared_weights)
    routed = jnp.stack(
        [
            jnp.dot(
                tables[s][1],
                returned[s].reshape(experts * capacity, model_width).astype(jnp.float32),
                precision=lax.Precision.HIGHEST,
            )
            for s in range(step_count)
        ]
    )
    return (shared + routed).astype(jnp.bfloat16)


def solution(mesh):
    placed = (
        P(None, "ep", None),
        P(None, "ep", None),
        P(None, "ep", None),
        P("ep", None, None),
        P("ep", None, None),
        P("ep", None, None),
        P(None, None, "ep"),
    )
    return jax.shard_map(
        shards, mesh=mesh, in_specs=placed, out_specs=P(None, "ep", None), check_vma=False
    )
```

```python
import jax
import jax.numpy as jnp
from jax import lax
from jax.sharding import PartitionSpec as P
from jax.experimental import pallas as pl
from jax.experimental.pallas import tpu as pltpu


def partner_2(block, axis, apart):
    count = lax.axis_size(axis)
    route = []
    for low in range(count):
        high = low | 1 << apart
        if high != low and high < count:
            route += [(low, high), (high, low)]
    return lax.ppermute(block, axis, route)


def ffn_kernel(x_ref, gate_ref, up_ref, down_ref, out_ref, total):
    step = pl.program_id(0)

    @pl.when(step == 0)
    def _():
        total[...] = jnp.zeros_like(total)

    rows = x_ref[...]
    gate_val = jnp.dot(rows, gate_ref[...], preferred_element_type=jnp.float32)
    up_val = jnp.dot(rows, up_ref[...], preferred_element_type=jnp.float32)
    hidden = (gate_val / (1.0 + jnp.exp(-gate_val)) * up_val).astype(jnp.bfloat16)
    total[...] += jnp.dot(hidden, down_ref[...], preferred_element_type=jnp.float32)

    @pl.when(step == pl.num_programs(0) - 1)
    def _():
        out_ref[...] = total[...].astype(out_ref.dtype)


def expert_rows(token_rows, w_gate, w_up, w_down, tile=256):
    row_count, model_width = token_rows.shape
    hidden_width = w_gate.shape[2]
    steps = hidden_width // tile
    flops = 6 * row_count * model_width * hidden_width
    weight_bytes = 3 * model_width * hidden_width * 2
    return pl.pallas_call(
        ffn_kernel,
        out_shape=jax.ShapeDtypeStruct((row_count, model_width), jnp.bfloat16),
        grid=(steps,),
        in_specs=[
            pl.BlockSpec((row_count, model_width), lambda f: (0, 0)),
            pl.BlockSpec((None, model_width, tile), lambda f: (0, 0, f)),
            pl.BlockSpec((None, model_width, tile), lambda f: (0, 0, f)),
            pl.BlockSpec((None, tile, model_width), lambda f: (0, f, 0)),
        ],
        out_specs=pl.BlockSpec((row_count, model_width), lambda f: (0, 0)),
        scratch_shapes=[pltpu.VMEM((row_count, model_width), jnp.float32)],
        compiler_params=pltpu.CompilerParams(
            dimension_semantics=("arbitrary",), vmem_limit_bytes=60 * 1024 * 1024
        ),
        cost_estimate=pl.CostEstimate(
            flops=flops,
            transcendentals=row_count * hidden_width,
            bytes_accessed=weight_bytes + 4 * row_count * model_width,
        ),
    )(token_rows, w_gate, w_up, w_down)


def route_tables(step_ids, step_weights, experts, capacity):
    row_count, top_count = step_ids.shape
    pair_count = row_count * top_count
    flat_ids = step_ids.reshape(pair_count)
    onehot = (flat_ids[:, None] == jnp.arange(experts, dtype=jnp.int32)[None, :]).astype(
        jnp.float32
    )
    earlier = (jnp.arange(pair_count)[:, None] > jnp.arange(pair_count)[None, :]).astype(
        jnp.float32
    )
    counts = jnp.dot(earlier, onehot, precision=lax.Precision.HIGHEST)
    slot_index = jnp.sum(counts * onehot, axis=1).astype(jnp.int32)
    position = flat_ids * capacity + slot_index
    placing = (
        position[:, None] == jnp.arange(experts * capacity, dtype=jnp.int32)[None, :]
    ).astype(jnp.float32)
    owner = (
        (jnp.arange(pair_count) // top_count)[:, None] == jnp.arange(row_count)[None, :]
    ).astype(jnp.float32)
    dispatch = jnp.dot(placing.T, owner, precision=lax.Precision.HIGHEST).astype(jnp.bfloat16)
    combine = jnp.dot(
        (owner * step_weights.reshape(pair_count)[:, None]).T,
        placing,
        precision=lax.Precision.HIGHEST,
    )
    return (dispatch, combine)


def join_halves(mine, partner, upper_side, axis_no):
    return jnp.where(
        upper_side,
        jnp.concatenate([partner, mine], axis=axis_no),
        jnp.concatenate([mine, partner], axis=axis_no),
    )


def shared_expert(tokens, shared_weights):
    my_index = lax.axis_index("ep")
    step_count, row_count, model_width = tokens.shape
    gathered = tokens
    for level in (2, 1, 0):
        partner = partner_2(gathered, "ep", level)
        gathered = join_halves(gathered, partner, my_index >> level & 1 == 1, 1)
    flat_rows = gathered.reshape(-1, model_width)
    gate_val = jnp.dot(flat_rows, shared_weights[0], preferred_element_type=jnp.float32)
    up_val = jnp.dot(flat_rows, shared_weights[1], preferred_element_type=jnp.float32)
    hidden = (jax.nn.silu(gate_val) * up_val).astype(jnp.bfloat16)
    partial_value = lax.dot_general(
        hidden, shared_weights[2], (((1,), (1,)), ((), ())), preferred_element_type=jnp.float32
    )
    partial_value = partial_value.reshape(step_count, 8 * row_count, model_width)
    for level in (0, 1, 2):
        half = partial_value.shape[1] // 2
        bit = my_index >> level & 1
        keep = lax.dynamic_slice_in_dim(partial_value, bit * half, half, 1)
        send = lax.dynamic_slice_in_dim(partial_value, (1 - bit) * half, half, 1)
        partial_value = keep + partner_2(send, "ep", level)
    return partial_value


def shards(tokens, expert_ids, combine_weights, w_gate, w_up, w_down, shared_weights):
    step_count, row_count, model_width = tokens.shape
    top_count = expert_ids.shape[2]
    device_count = lax.axis_size("ep")
    experts = w_gate.shape[0] * device_count
    capacity = max(2, row_count * top_count * 2 // experts)
    tables = [
        route_tables(expert_ids[s], combine_weights[s], experts, capacity)
        for s in range(step_count)
    ]
    outgoing = jnp.stack(
        [
            jnp.dot(tables[s][0], tokens[s], preferred_element_type=jnp.float32)
            .astype(jnp.bfloat16)
            .reshape(experts, capacity, model_width)
            for s in range(step_count)
        ]
    )
    received = lax.all_to_all(outgoing, "ep", split_axis=1, concat_axis=1, tiled=True)
    returned = lax.all_to_all(
        expert_rows(received.reshape(-1, model_width), w_gate, w_up, w_down).reshape(
            received.shape
        ),
        "ep",
        split_axis=1,
        concat_axis=1,
        tiled=True,
    )
    shared = shared_expert(tokens, shared_weights)
    routed = jnp.stack(
        [
            jnp.dot(
                tables[s][1],
                returned[s].reshape(experts * capacity, model_width).astype(jnp.float32),
                precision=lax.Precision.HIGHEST,
            )
            for s in range(step_count)
        ]
    )
    return (shared + routed).astype(jnp.bfloat16)


def solution(mesh):
    placed = (
        P(None, "ep", None),
        P(None, "ep", None),
        P(None, "ep", None),
        P("ep", None, None),
        P("ep", None, None),
        P("ep", None, None),
        P(None, None, "ep"),
    )
    return jax.shard_map(
        shards, mesh=mesh, in_specs=placed, out_specs=P(None, "ep", None), check_vma=False
    )
```

```python
import jax
import jax.numpy as jnp
from jax import lax
from jax.sharding import PartitionSpec as P
from jax.experimental import pallas as pl
from jax.experimental.pallas import tpu as pltpu


def partner_2(block, axis, apart):
    count = lax.axis_size(axis)
    route = []
    for low in range(count):
        high = low | 1 << apart
        if high != low and high < count:
            route += [(low, high), (high, low)]
    return lax.ppermute(block, axis, route)


def ffn_kernel(x_ref, gate_ref, up_ref, down_ref, out_ref, total):
    step = pl.program_id(0)

    @pl.when(step == 0)
    def _():
        total[...] = jnp.zeros_like(total)

    rows = x_ref[...]
    gate_val = jnp.dot(rows, gate_ref[...], preferred_element_type=jnp.float32)
    up_val = jnp.dot(rows, up_ref[...], preferred_element_type=jnp.float32)
    hidden = (gate_val / (1.0 + jnp.exp(-gate_val)) * up_val).astype(jnp.bfloat16)
    total[...] += jnp.dot(hidden, down_ref[...], preferred_element_type=jnp.float32)

    @pl.when(step == pl.num_programs(0) - 1)
    def _():
        out_ref[...] = total[...].astype(out_ref.dtype)


def expert_rows(token_rows, w_gate, w_up, w_down, tile=256):
    row_count, model_width = token_rows.shape
    hidden_width = w_gate.shape[2]
    steps = hidden_width // tile
    flops = 6 * row_count * model_width * hidden_width
    weight_bytes = 3 * model_width * hidden_width * 2
    return pl.pallas_call(
        ffn_kernel,
        out_shape=jax.ShapeDtypeStruct((row_count, model_width), jnp.bfloat16),
        grid=(steps,),
        in_specs=[
            pl.BlockSpec((row_count, model_width), lambda f: (0, 0)),
            pl.BlockSpec((None, model_width, tile), lambda f: (0, 0, f)),
            pl.BlockSpec((None, model_width, tile), lambda f: (0, 0, f)),
            pl.BlockSpec((None, tile, model_width), lambda f: (0, f, 0)),
        ],
        out_specs=pl.BlockSpec((row_count, model_width), lambda f: (0, 0)),
        scratch_shapes=[pltpu.VMEM((row_count, model_width), jnp.float32)],
        compiler_params=pltpu.CompilerParams(
            dimension_semantics=("arbitrary",), vmem_limit_bytes=60 * 1024 * 1024
        ),
        cost_estimate=pl.CostEstimate(
            flops=flops,
            transcendentals=row_count * hidden_width,
            bytes_accessed=weight_bytes + 4 * row_count * model_width,
        ),
    )(token_rows, w_gate, w_up, w_down)


def route_tables(step_ids, step_weights, experts, capacity):
    row_count, top_count = step_ids.shape
    pair_count = row_count * top_count
    flat_ids = step_ids.reshape(pair_count)
    onehot = (flat_ids[:, None] == jnp.arange(experts, dtype=jnp.int32)[None, :]).astype(
        jnp.float32
    )
    earlier = (jnp.arange(pair_count)[:, None] > jnp.arange(pair_count)[None, :]).astype(
        jnp.float32
    )
    counts = jnp.dot(earlier, onehot, precision=lax.Precision.HIGHEST)
    slot_index = jnp.sum(counts * onehot, axis=1).astype(jnp.int32)
    position = flat_ids * capacity + slot_index
    placing = (
        position[:, None] == jnp.arange(experts * capacity, dtype=jnp.int32)[None, :]
    ).astype(jnp.float32)
    owner = (
        (jnp.arange(pair_count) // top_count)[:, None] == jnp.arange(row_count)[None, :]
    ).astype(jnp.float32)
    dispatch = jnp.dot(placing.T, owner, precision=lax.Precision.HIGHEST).astype(jnp.bfloat16)
    combine = jnp.dot(
        (owner * step_weights.reshape(pair_count)[:, None]).T,
        placing,
        precision=lax.Precision.HIGHEST,
    )
    return (dispatch, combine)


def join_halves(mine, partner, upper_side, axis_no):
    return jnp.where(
        upper_side,
        jnp.concatenate([partner, mine], axis=axis_no),
        jnp.concatenate([mine, partner], axis=axis_no),
    )


def shared_expert(tokens, shared_weights):
    my_index = lax.axis_index("ep")
    step_count, row_count, model_width = tokens.shape
    gathered = tokens
    for level in (2, 1, 0):
        partner = partner_2(gathered, "ep", level)
        gathered = join_halves(gathered, partner, my_index >> level & 1 == 1, 1)
    flat_rows = gathered.reshape(-1, model_width)
    gate_val = jnp.dot(flat_rows, shared_weights[0], preferred_element_type=jnp.float32)
    up_val = jnp.dot(flat_rows, shared_weights[1], preferred_element_type=jnp.float32)
    hidden = (jax.nn.silu(gate_val) * up_val).astype(jnp.bfloat16)
    partial_value = lax.dot_general(
        hidden, shared_weights[2], (((1,), (1,)), ((), ())), preferred_element_type=jnp.float32
    )
    partial_value = partial_value.reshape(step_count, 8 * row_count, model_width)
    for level in (0, 1, 2):
        half = partial_value.shape[1] // 2
        bit = my_index >> level & 1
        keep = lax.dynamic_slice_in_dim(partial_value, bit * half, half, 1)
        send = lax.dynamic_slice_in_dim(partial_value, (1 - bit) * half, half, 1)
        partial_value = keep + partner_2(send, "ep", level)
    return partial_value


def shards(tokens, expert_ids, combine_weights, w_gate, w_up, w_down, shared_weights):
    step_count, row_count, model_width = tokens.shape
    top_count = expert_ids.shape[2]
    device_count = lax.axis_size("ep")
    experts = w_gate.shape[0] * device_count
    capacity = max(2, row_count * top_count * 2 // experts)
    routed_steps = []
    for s in range(step_count):
        dispatch, combine = route_tables(expert_ids[s], combine_weights[s], experts, capacity)
        outgoing = (
            jnp.dot(dispatch, tokens[s], preferred_element_type=jnp.float32)
            .astype(jnp.bfloat16)
            .reshape(experts, capacity, model_width)
        )
        received = lax.all_to_all(outgoing, "ep", split_axis=0, concat_axis=0, tiled=True)
        expert_out = expert_rows(
            received.reshape(-1, model_width), w_gate, w_up, w_down
        ).reshape(received.shape)
        returned = lax.all_to_all(expert_out, "ep", split_axis=0, concat_axis=0, tiled=True)
        routed_steps.append(
            jnp.dot(
                combine,
                returned.reshape(experts * capacity, model_width).astype(jnp.float32),
                precision=lax.Precision.HIGHEST,
            )
        )
    shared = shared_expert(tokens, shared_weights)
    routed = jnp.stack(routed_steps)
    return (shared + routed).astype(jnp.bfloat16)


def solution(mesh):
    placed = (
        P(None, "ep", None),
        P(None, "ep", None),
        P(None, "ep", None),
        P("ep", None, None),
        P("ep", None, None),
        P("ep", None, None),
        P(None, None, "ep"),
    )
    return jax.shard_map(
        shards, mesh=mesh, in_specs=placed, out_specs=P(None, "ep", None), check_vma=False
    )
```

```python
import jax
import jax.numpy as jnp
from jax import lax
from jax.sharding import PartitionSpec as P
from jax.experimental import pallas as pl
from jax.experimental.pallas import tpu as pltpu


def partner_2(block, axis, apart):
    count = lax.axis_size(axis)
    route = []
    for low in range(count):
        high = low | 1 << apart
        if high != low and high < count:
            route += [(low, high), (high, low)]
    return lax.ppermute(block, axis, route)


def ffn_kernel(x_ref, gate_ref, up_ref, down_ref, out_ref, total):
    step = pl.program_id(0)

    @pl.when(step == 0)
    def _():
        total[...] = jnp.zeros_like(total)

    rows = x_ref[...].reshape(-1, x_ref.shape[-1])
    gate_val = jnp.dot(rows, gate_ref[...], preferred_element_type=jnp.float32)
    up_val = jnp.dot(rows, up_ref[...], preferred_element_type=jnp.float32)
    hidden = (gate_val / (1.0 + jnp.exp(-gate_val)) * up_val).astype(jnp.bfloat16)
    total[...] += jnp.dot(hidden, down_ref[...], preferred_element_type=jnp.float32)

    @pl.when(step == pl.num_programs(0) - 1)
    def _():
        out_ref[...] = total[...].astype(out_ref.dtype).reshape(out_ref.shape)


def expert_rows(token_block, w_gate, w_up, w_down, tile=256):
    model_width = token_block.shape[-1]
    row_count = token_block.size // model_width
    hidden_width = w_gate.shape[2]
    steps = hidden_width // tile
    flops = 6 * row_count * model_width * hidden_width
    weight_bytes = 3 * model_width * hidden_width * 2
    whole = (0,) * token_block.ndim
    return pl.pallas_call(
        ffn_kernel,
        out_shape=jax.ShapeDtypeStruct(token_block.shape, jnp.bfloat16),
        grid=(steps,),
        in_specs=[
            pl.BlockSpec(token_block.shape, lambda f: whole),
            pl.BlockSpec((None, model_width, tile), lambda f: (0, 0, f)),
            pl.BlockSpec((None, model_width, tile), lambda f: (0, 0, f)),
            pl.BlockSpec((None, tile, model_width), lambda f: (0, f, 0)),
        ],
        out_specs=pl.BlockSpec(token_block.shape, lambda f: whole),
        scratch_shapes=[pltpu.VMEM((row_count, model_width), jnp.float32)],
        compiler_params=pltpu.CompilerParams(
            dimension_semantics=("arbitrary",), vmem_limit_bytes=60 * 1024 * 1024
        ),
        cost_estimate=pl.CostEstimate(
            flops=flops,
            transcendentals=row_count * hidden_width,
            bytes_accessed=weight_bytes + 4 * row_count * model_width,
        ),
    )(token_block, w_gate, w_up, w_down)


def route_tables(step_ids, step_weights, experts, capacity):
    row_count, top_count = step_ids.shape
    pair_count = row_count * top_count
    flat_ids = step_ids.reshape(pair_count)
    onehot = (flat_ids[:, None] == jnp.arange(experts, dtype=jnp.int32)[None, :]).astype(
        jnp.float32
    )
    earlier = (jnp.arange(pair_count)[:, None] > jnp.arange(pair_count)[None, :]).astype(
        jnp.float32
    )
    counts = jnp.dot(earlier, onehot, precision=lax.Precision.HIGHEST)
    slot_index = jnp.sum(counts * onehot, axis=1).astype(jnp.int32)
    position = flat_ids * capacity + slot_index
    placing = (
        position[:, None] == jnp.arange(experts * capacity, dtype=jnp.int32)[None, :]
    ).astype(jnp.float32)
    owner = (
        (jnp.arange(pair_count) // top_count)[:, None] == jnp.arange(row_count)[None, :]
    ).astype(jnp.float32)
    dispatch = jnp.dot(placing.T, owner, precision=lax.Precision.HIGHEST).astype(jnp.bfloat16)
    combine = jnp.dot(
        (owner * step_weights.reshape(pair_count)[:, None]).T,
        placing,
        precision=lax.Precision.HIGHEST,
    )
    return (dispatch, combine)


def join_halves(mine, partner, upper_side, axis_no):
    return jnp.where(
        upper_side,
        jnp.concatenate([partner, mine], axis=axis_no),
        jnp.concatenate([mine, partner], axis=axis_no),
    )


def shared_expert(tokens, shared_weights):
    my_index = lax.axis_index("ep")
    step_count, row_count, model_width = tokens.shape
    gathered = tokens
    for level in (2, 1, 0):
        partner = partner_2(gathered, "ep", level)
        gathered = join_halves(gathered, partner, my_index >> level & 1 == 1, 1)
    flat_rows = gathered.reshape(-1, model_width)
    gate_val = jnp.dot(flat_rows, shared_weights[0], preferred_element_type=jnp.float32)
    up_val = jnp.dot(flat_rows, shared_weights[1], preferred_element_type=jnp.float32)
    hidden = (jax.nn.silu(gate_val) * up_val).astype(jnp.bfloat16)
    partial_value = lax.dot_general(
        hidden, shared_weights[2], (((1,), (1,)), ((), ())), preferred_element_type=jnp.float32
    )
    partial_value = partial_value.reshape(step_count, 8 * row_count, model_width)
    for level in (0, 1, 2):
        half = partial_value.shape[1] // 2
        bit = my_index >> level & 1
        keep = lax.dynamic_slice_in_dim(partial_value, bit * half, half, 1)
        send = lax.dynamic_slice_in_dim(partial_value, (1 - bit) * half, half, 1)
        partial_value = keep + partner_2(send, "ep", level)
    return partial_value


def shards(tokens, expert_ids, combine_weights, w_gate, w_up, w_down, shared_weights):
    step_count, row_count, model_width = tokens.shape
    top_count = expert_ids.shape[2]
    device_count = lax.axis_size("ep")
    experts = w_gate.shape[0] * device_count
    capacity = max(2, row_count * top_count * 2 // experts)
    routed_steps = []
    for s in range(step_count):
        dispatch, combine = route_tables(expert_ids[s], combine_weights[s], experts, capacity)
        outgoing = jnp.einsum(
            "ect,td->ecd",
            dispatch.reshape(experts, capacity, row_count),
            tokens[s],
            preferred_element_type=jnp.float32,
        ).astype(jnp.bfloat16)
        received = lax.all_to_all(outgoing, "ep", split_axis=0, concat_axis=0, tiled=True)
        expert_out = expert_rows(received, w_gate, w_up, w_down)
        returned = lax.all_to_all(expert_out, "ep", split_axis=0, concat_axis=0, tiled=True)
        routed_steps.append(
            jnp.einsum(
                "tec,ecd->td",
                combine.reshape(row_count, experts, capacity),
                returned.astype(jnp.float32),
                precision=lax.Precision.HIGHEST,
            )
        )
    shared = shared_expert(tokens, shared_weights)
    routed = jnp.stack(routed_steps)
    return (shared + routed).astype(jnp.bfloat16)


def solution(mesh):
    placed = (
        P(None, "ep", None),
        P(None, "ep", None),
        P(None, "ep", None),
        P("ep", None, None),
        P("ep", None, None),
        P("ep", None, None),
        P(None, None, "ep"),
    )
    return jax.shard_map(
        shards, mesh=mesh, in_specs=placed, out_specs=P(None, "ep", None), check_vma=False
    )
```

```python
import jax
import jax.numpy as jnp
from jax import lax
from jax.sharding import PartitionSpec as P
from jax.experimental import pallas as pl
from jax.experimental.pallas import tpu as pltpu


def partner_2(block, axis, apart):
    count = lax.axis_size(axis)
    route = []
    for low in range(count):
        high = low | 1 << apart
        if high != low and high < count:
            route += [(low, high), (high, low)]
    return lax.ppermute(block, axis, route)


def ffn_kernel(x_ref, gate_ref, up_ref, down_ref, out_ref, total):
    step = pl.program_id(0)

    @pl.when(step == 0)
    def _():
        total[...] = jnp.zeros_like(total)

    rows = x_ref[...].reshape(-1, x_ref.shape[-1])
    gate_val = jnp.dot(rows, gate_ref[...], preferred_element_type=jnp.float32)
    up_val = jnp.dot(rows, up_ref[...], preferred_element_type=jnp.float32)
    hidden = (gate_val / (1.0 + jnp.exp(-gate_val)) * up_val).astype(jnp.bfloat16)
    total[...] += jnp.dot(hidden, down_ref[...], preferred_element_type=jnp.float32)

    @pl.when(step == pl.num_programs(0) - 1)
    def _():
        out_ref[...] = total[...].astype(out_ref.dtype).reshape(out_ref.shape)


def expert_rows(token_block, w_gate, w_up, w_down, tile=256):
    model_width = token_block.shape[-1]
    row_count = token_block.size // model_width
    hidden_width = w_gate.shape[2]
    steps = hidden_width // tile
    flops = 6 * row_count * model_width * hidden_width
    weight_bytes = 3 * model_width * hidden_width * 2
    whole = (0,) * token_block.ndim
    return pl.pallas_call(
        ffn_kernel,
        out_shape=jax.ShapeDtypeStruct(token_block.shape, jnp.bfloat16),
        grid=(steps,),
        in_specs=[
            pl.BlockSpec(token_block.shape, lambda f: whole),
            pl.BlockSpec((None, model_width, tile), lambda f: (0, 0, f)),
            pl.BlockSpec((None, model_width, tile), lambda f: (0, 0, f)),
            pl.BlockSpec((None, tile, model_width), lambda f: (0, f, 0)),
        ],
        out_specs=pl.BlockSpec(token_block.shape, lambda f: whole),
        scratch_shapes=[pltpu.VMEM((row_count, model_width), jnp.float32)],
        compiler_params=pltpu.CompilerParams(
            dimension_semantics=("arbitrary",), vmem_limit_bytes=60 * 1024 * 1024
        ),
        cost_estimate=pl.CostEstimate(
            flops=flops,
            transcendentals=row_count * hidden_width,
            bytes_accessed=weight_bytes + 4 * row_count * model_width,
        ),
    )(token_block, w_gate, w_up, w_down)


def route_tables(step_ids, step_weights, experts, capacity):
    row_count, top_count = step_ids.shape
    pair_count = row_count * top_count
    flat_ids = step_ids.reshape(pair_count)
    onehot = (flat_ids[:, None] == jnp.arange(experts, dtype=jnp.int32)[None, :]).astype(
        jnp.float32
    )
    earlier = (jnp.arange(pair_count)[:, None] > jnp.arange(pair_count)[None, :]).astype(
        jnp.float32
    )
    counts = jnp.dot(earlier, onehot, precision=lax.Precision.HIGHEST)
    slot_index = jnp.sum(counts * onehot, axis=1).astype(jnp.int32)
    position = flat_ids * capacity + slot_index
    placing = (
        position[:, None] == jnp.arange(experts * capacity, dtype=jnp.int32)[None, :]
    ).astype(jnp.float32)
    owner = (
        (jnp.arange(pair_count) // top_count)[:, None] == jnp.arange(row_count)[None, :]
    ).astype(jnp.float32)
    dispatch = jnp.dot(placing.T, owner, precision=lax.Precision.HIGHEST).astype(jnp.bfloat16)
    combine = jnp.dot(
        (owner * step_weights.reshape(pair_count)[:, None]).T,
        placing,
        precision=lax.Precision.HIGHEST,
    )
    return (dispatch, combine)


def join_halves(mine, partner, upper_side, axis_no):
    return jnp.where(
        upper_side,
        jnp.concatenate([partner, mine], axis=axis_no),
        jnp.concatenate([mine, partner], axis=axis_no),
    )


def shared_expert(tokens, shared_weights):
    my_index = lax.axis_index("ep")
    step_count, row_count, model_width = tokens.shape
    gathered = tokens
    for level in (2, 1, 0):
        partner = partner_2(gathered, "ep", level)
        gathered = join_halves(gathered, partner, my_index >> level & 1 == 1, 1)
    flat_rows = gathered.reshape(-1, model_width)
    gate_val = jnp.dot(flat_rows, shared_weights[0], preferred_element_type=jnp.float32)
    up_val = jnp.dot(flat_rows, shared_weights[1], preferred_element_type=jnp.float32)
    hidden = (jax.nn.silu(gate_val) * up_val).astype(jnp.bfloat16)
    partial_value = lax.dot_general(
        hidden, shared_weights[2], (((1,), (1,)), ((), ())), preferred_element_type=jnp.float32
    )
    partial_value = partial_value.reshape(step_count, 8 * row_count, model_width)
    for level in (0, 1, 2):
        half = partial_value.shape[1] // 2
        bit = my_index >> level & 1
        keep = lax.dynamic_slice_in_dim(partial_value, bit * half, half, 1)
        send = lax.dynamic_slice_in_dim(partial_value, (1 - bit) * half, half, 1)
        partial_value = keep + partner_2(send.astype(jnp.bfloat16), "ep", level).astype(
            jnp.float32
        )
    return partial_value


def shards(tokens, expert_ids, combine_weights, w_gate, w_up, w_down, shared_weights):
    step_count, row_count, model_width = tokens.shape
    top_count = expert_ids.shape[2]
    device_count = lax.axis_size("ep")
    experts = w_gate.shape[0] * device_count
    capacity = max(2, row_count * top_count * 2 // experts)
    payloads = []
    combines = []
    for s in range(step_count):
        dispatch, combine = route_tables(expert_ids[s], combine_weights[s], experts, capacity)
        payloads.append(
            jnp.einsum(
                "ect,td->ecd",
                dispatch.reshape(experts, capacity, row_count),
                tokens[s],
                preferred_element_type=jnp.float32,
            ).astype(jnp.bfloat16)
        )
        combines.append(combine)
    routed_steps = []
    for s in range(step_count):
        received = lax.all_to_all(payloads[s], "ep", split_axis=0, concat_axis=0, tiled=True)
        expert_out = expert_rows(received, w_gate, w_up, w_down)
        returned = lax.all_to_all(expert_out, "ep", split_axis=0, concat_axis=0, tiled=True)
        routed_steps.append(
            jnp.einsum(
                "tec,ecd->td",
                combines[s].reshape(row_count, experts, capacity),
                returned.astype(jnp.float32),
                precision=lax.Precision.HIGHEST,
            )
        )
    later_tokens = lax.optimization_barrier((tokens, *payloads))[0]
    shared = shared_expert(later_tokens, shared_weights)
    routed = jnp.stack(routed_steps)
    return (shared + routed).astype(jnp.bfloat16)


def solution(mesh):
    placed = (
        P(None, "ep", None),
        P(None, "ep", None),
        P(None, "ep", None),
        P("ep", None, None),
        P("ep", None, None),
        P("ep", None, None),
        P(None, None, "ep"),
    )
    return jax.shard_map(
        shards, mesh=mesh, in_specs=placed, out_specs=P(None, "ep", None), check_vma=False
    )
```

```python
import jax
import jax.numpy as jnp
from jax import lax
from jax.sharding import PartitionSpec as P
from jax.experimental import pallas as pl
from jax.experimental.pallas import tpu as pltpu


def partner_2(block, axis, apart):
    count = lax.axis_size(axis)
    route = []
    for low in range(count):
        high = low | 1 << apart
        if high != low and high < count:
            route += [(low, high), (high, low)]
    return lax.ppermute(block, axis, route)


def ffn_kernel(x_ref, gate_ref, up_ref, down_ref, out_ref, total):
    step = pl.program_id(0)

    @pl.when(step == 0)
    def _():
        total[...] = jnp.zeros_like(total)

    rows = x_ref[...].reshape(-1, x_ref.shape[-1])
    gate_val = jnp.dot(rows, gate_ref[...], preferred_element_type=jnp.float32)
    up_val = jnp.dot(rows, up_ref[...], preferred_element_type=jnp.float32)
    hidden = (gate_val / (1.0 + jnp.exp(-gate_val)) * up_val).astype(jnp.bfloat16)
    total[...] += jnp.dot(hidden, down_ref[...], preferred_element_type=jnp.float32)

    @pl.when(step == pl.num_programs(0) - 1)
    def _():
        out_ref[...] = total[...].astype(out_ref.dtype).reshape(out_ref.shape)


def expert_rows(token_block, w_gate, w_up, w_down, tile=256):
    model_width = token_block.shape[-1]
    row_count = token_block.size // model_width
    hidden_width = w_gate.shape[2]
    steps = hidden_width // tile
    flops = 6 * row_count * model_width * hidden_width
    weight_bytes = 3 * model_width * hidden_width * 2
    whole = (0,) * token_block.ndim
    return pl.pallas_call(
        ffn_kernel,
        out_shape=jax.ShapeDtypeStruct(token_block.shape, jnp.bfloat16),
        grid=(steps,),
        in_specs=[
            pl.BlockSpec(token_block.shape, lambda f: whole),
            pl.BlockSpec((None, model_width, tile), lambda f: (0, 0, f)),
            pl.BlockSpec((None, model_width, tile), lambda f: (0, 0, f)),
            pl.BlockSpec((None, tile, model_width), lambda f: (0, f, 0)),
        ],
        out_specs=pl.BlockSpec(token_block.shape, lambda f: whole),
        scratch_shapes=[pltpu.VMEM((row_count, model_width), jnp.float32)],
        compiler_params=pltpu.CompilerParams(
            dimension_semantics=("arbitrary",), vmem_limit_bytes=60 * 1024 * 1024
        ),
        cost_estimate=pl.CostEstimate(
            flops=flops,
            transcendentals=row_count * hidden_width,
            bytes_accessed=weight_bytes + 4 * row_count * model_width,
        ),
    )(token_block, w_gate, w_up, w_down)


def route_tables(step_ids, step_weights, experts, capacity):
    row_count, top_count = step_ids.shape
    pair_count = row_count * top_count
    flat_ids = step_ids.reshape(pair_count)
    onehot = (flat_ids[:, None] == jnp.arange(experts, dtype=jnp.int32)[None, :]).astype(
        jnp.float32
    )
    earlier = (jnp.arange(pair_count)[:, None] > jnp.arange(pair_count)[None, :]).astype(
        jnp.float32
    )
    counts = jnp.dot(earlier, onehot, precision=lax.Precision.HIGHEST)
    slot_index = jnp.sum(counts * onehot, axis=1).astype(jnp.int32)
    position = flat_ids * capacity + slot_index
    placing = (
        position[:, None] == jnp.arange(experts * capacity, dtype=jnp.int32)[None, :]
    ).astype(jnp.float32)
    owner = (
        (jnp.arange(pair_count) // top_count)[:, None] == jnp.arange(row_count)[None, :]
    ).astype(jnp.float32)
    dispatch = jnp.dot(placing.T, owner, precision=lax.Precision.HIGHEST).astype(jnp.bfloat16)
    combine = jnp.dot(
        (owner * step_weights.reshape(pair_count)[:, None]).T,
        placing,
        precision=lax.Precision.HIGHEST,
    )
    return (dispatch, combine)


def join_halves(mine, partner, upper_side, axis_no):
    return jnp.where(
        upper_side,
        jnp.concatenate([partner, mine], axis=axis_no),
        jnp.concatenate([mine, partner], axis=axis_no),
    )


def shared_expert(tokens, shared_weights):
    step_count, row_count, model_width = tokens.shape
    count = lax.axis_size("ep")
    groups = [list(range(g, g + 8)) for g in range(0, count, 8)]
    gathered = lax.all_gather(tokens, "ep", axis=1, tiled=True, axis_index_groups=groups)
    flat_rows = gathered.reshape(-1, model_width)
    gate_val = jnp.dot(flat_rows, shared_weights[0], preferred_element_type=jnp.float32)
    up_val = jnp.dot(flat_rows, shared_weights[1], preferred_element_type=jnp.float32)
    hidden = (jax.nn.silu(gate_val) * up_val).astype(jnp.bfloat16)
    partial_value = lax.dot_general(
        hidden, shared_weights[2], (((1,), (1,)), ((), ())), preferred_element_type=jnp.float32
    )
    partial_value = partial_value.reshape(step_count, 8 * row_count, model_width)
    return lax.psum_scatter(
        partial_value, "ep", scatter_dimension=1, tiled=True, axis_index_groups=groups
    )


def shards(tokens, expert_ids, combine_weights, w_gate, w_up, w_down, shared_weights):
    step_count, row_count, model_width = tokens.shape
    top_count = expert_ids.shape[2]
    device_count = lax.axis_size("ep")
    experts = w_gate.shape[0] * device_count
    capacity = max(2, row_count * top_count * 2 // experts)
    payloads = []
    combines = []
    for s in range(step_count):
        dispatch, combine = route_tables(expert_ids[s], combine_weights[s], experts, capacity)
        payloads.append(
            jnp.einsum(
                "ect,td->ecd",
                dispatch.reshape(experts, capacity, row_count),
                tokens[s],
                preferred_element_type=jnp.float32,
            ).astype(jnp.bfloat16)
        )
        combines.append(combine)
    routed_steps = []
    for s in range(step_count):
        received = lax.all_to_all(payloads[s], "ep", split_axis=0, concat_axis=0, tiled=True)
        expert_out = expert_rows(received, w_gate, w_up, w_down)
        returned = lax.all_to_all(expert_out, "ep", split_axis=0, concat_axis=0, tiled=True)
        routed_steps.append(
            jnp.einsum(
                "tec,ecd->td",
                combines[s].reshape(row_count, experts, capacity),
                returned.astype(jnp.float32),
                precision=lax.Precision.HIGHEST,
            )
        )
    shared = shared_expert(tokens, shared_weights)
    routed = jnp.stack(routed_steps)
    return (shared + routed).astype(jnp.bfloat16)


def solution(mesh):
    placed = (
        P(None, "ep", None),
        P(None, "ep", None),
        P(None, "ep", None),
        P("ep", None, None),
        P("ep", None, None),
        P("ep", None, None),
        P(None, None, "ep"),
    )
    return jax.shard_map(
        shards, mesh=mesh, in_specs=placed, out_specs=P(None, "ep", None), check_vma=False
    )
```

```python
import jax
import jax.numpy as jnp
from jax import lax
from jax.sharding import PartitionSpec as P
from jax.experimental import pallas as pl
from jax.experimental.pallas import tpu as pltpu


def partner_2(block, axis, apart):
    count = lax.axis_size(axis)
    route = []
    for low in range(count):
        high = low | 1 << apart
        if high != low and high < count:
            route += [(low, high), (high, low)]
    return lax.ppermute(block, axis, route)


def ffn_kernel(x_ref, gate_ref, up_ref, down_ref, out_ref, total):
    step = pl.program_id(0)

    @pl.when(step == 0)
    def _():
        total[...] = jnp.zeros_like(total)

    rows = x_ref[...].reshape(-1, x_ref.shape[-1])
    gate_val = jnp.dot(rows, gate_ref[...], preferred_element_type=jnp.float32)
    up_val = jnp.dot(rows, up_ref[...], preferred_element_type=jnp.float32)
    hidden = (gate_val / (1.0 + jnp.exp(-gate_val)) * up_val).astype(jnp.bfloat16)
    total[...] += jnp.dot(hidden, down_ref[...], preferred_element_type=jnp.float32)

    @pl.when(step == pl.num_programs(0) - 1)
    def _():
        out_ref[...] = total[...].astype(out_ref.dtype).reshape(out_ref.shape)


def expert_rows(token_block, w_gate, w_up, w_down, tile=256):
    model_width = token_block.shape[-1]
    row_count = token_block.size // model_width
    hidden_width = w_gate.shape[2]
    steps = hidden_width // tile
    flops = 6 * row_count * model_width * hidden_width
    weight_bytes = 3 * model_width * hidden_width * 2
    whole = (0,) * token_block.ndim
    return pl.pallas_call(
        ffn_kernel,
        out_shape=jax.ShapeDtypeStruct(token_block.shape, jnp.bfloat16),
        grid=(steps,),
        in_specs=[
            pl.BlockSpec(token_block.shape, lambda f: whole),
            pl.BlockSpec((None, model_width, tile), lambda f: (0, 0, f)),
            pl.BlockSpec((None, model_width, tile), lambda f: (0, 0, f)),
            pl.BlockSpec((None, tile, model_width), lambda f: (0, f, 0)),
        ],
        out_specs=pl.BlockSpec(token_block.shape, lambda f: whole),
        scratch_shapes=[pltpu.VMEM((row_count, model_width), jnp.float32)],
        compiler_params=pltpu.CompilerParams(
            dimension_semantics=("arbitrary",), vmem_limit_bytes=60 * 1024 * 1024
        ),
        cost_estimate=pl.CostEstimate(
            flops=flops,
            transcendentals=row_count * hidden_width,
            bytes_accessed=weight_bytes + 4 * row_count * model_width,
        ),
    )(token_block, w_gate, w_up, w_down)


def dispatch_kernel(select_ref, token_ref, out_ref):
    picked = jnp.dot(select_ref[...], token_ref[...], preferred_element_type=jnp.float32)
    out_ref[...] = picked.astype(out_ref.dtype).reshape(out_ref.shape)


def dispatch_rows(select, step_tokens, experts, capacity):
    model_width = step_tokens.shape[-1]
    return pl.pallas_call(
        dispatch_kernel,
        out_shape=jax.ShapeDtypeStruct((experts, capacity, model_width), step_tokens.dtype),
        in_specs=[
            pl.BlockSpec(memory_space=pltpu.VMEM),
            pl.BlockSpec(memory_space=pltpu.VMEM),
        ],
        out_specs=pl.BlockSpec(memory_space=pltpu.VMEM),
    )(select, step_tokens)


def route_tables(step_ids, step_weights, experts, capacity):
    row_count, top_count = step_ids.shape
    pair_count = row_count * top_count
    flat_ids = step_ids.reshape(pair_count)
    onehot = (flat_ids[:, None] == jnp.arange(experts, dtype=jnp.int32)[None, :]).astype(
        jnp.float32
    )
    earlier = (jnp.arange(pair_count)[:, None] > jnp.arange(pair_count)[None, :]).astype(
        jnp.float32
    )
    counts = jnp.dot(earlier, onehot, precision=lax.Precision.HIGHEST)
    slot_index = jnp.sum(counts * onehot, axis=1).astype(jnp.int32)
    position = flat_ids * capacity + slot_index
    placing = (
        position[:, None] == jnp.arange(experts * capacity, dtype=jnp.int32)[None, :]
    ).astype(jnp.float32)
    owner = (
        (jnp.arange(pair_count) // top_count)[:, None] == jnp.arange(row_count)[None, :]
    ).astype(jnp.float32)
    dispatch = jnp.dot(placing.T, owner, precision=lax.Precision.HIGHEST).astype(jnp.bfloat16)
    combine = jnp.dot(
        (owner * step_weights.reshape(pair_count)[:, None]).T,
        placing,
        precision=lax.Precision.HIGHEST,
    )
    return (dispatch, combine)


def join_halves(mine, partner, upper_side, axis_no):
    return jnp.where(
        upper_side,
        jnp.concatenate([partner, mine], axis=axis_no),
        jnp.concatenate([mine, partner], axis=axis_no),
    )


def shared_expert(tokens, shared_weights):
    my_index = lax.axis_index("ep")
    step_count, row_count, model_width = tokens.shape
    gathered = tokens
    for level in (2, 1, 0):
        partner = partner_2(gathered, "ep", level)
        gathered = join_halves(gathered, partner, my_index >> level & 1 == 1, 1)
    flat_rows = gathered.reshape(-1, model_width)
    gate_val = jnp.dot(flat_rows, shared_weights[0], preferred_element_type=jnp.float32)
    up_val = jnp.dot(flat_rows, shared_weights[1], preferred_element_type=jnp.float32)
    hidden = (jax.nn.silu(gate_val) * up_val).astype(jnp.bfloat16)
    partial_value = lax.dot_general(
        hidden, shared_weights[2], (((1,), (1,)), ((), ())), preferred_element_type=jnp.float32
    )
    partial_value = partial_value.reshape(step_count, 8 * row_count, model_width)
    for level in (0, 1, 2):
        half = partial_value.shape[1] // 2
        bit = my_index >> level & 1
        keep = lax.dynamic_slice_in_dim(partial_value, bit * half, half, 1)
        send = lax.dynamic_slice_in_dim(partial_value, (1 - bit) * half, half, 1)
        partial_value = keep + partner_2(send, "ep", level)
    return partial_value


def shards(tokens, expert_ids, combine_weights, w_gate, w_up, w_down, shared_weights):
    step_count, row_count, model_width = tokens.shape
    top_count = expert_ids.shape[2]
    device_count = lax.axis_size("ep")
    experts = w_gate.shape[0] * device_count
    capacity = max(2, row_count * top_count * 2 // experts)
    payloads = []
    combines = []
    for s in range(step_count):
        dispatch, combine = route_tables(expert_ids[s], combine_weights[s], experts, capacity)
        payloads.append(dispatch_rows(dispatch, tokens[s], experts, capacity))
        combines.append(combine)
    routed_steps = []
    for s in range(step_count):
        received = lax.all_to_all(payloads[s], "ep", split_axis=0, concat_axis=0, tiled=True)
        expert_out = expert_rows(received, w_gate, w_up, w_down)
        returned = lax.all_to_all(expert_out, "ep", split_axis=0, concat_axis=0, tiled=True)
        routed_steps.append(
            jnp.einsum(
                "tec,ecd->td",
                combines[s].reshape(row_count, experts, capacity),
                returned.astype(jnp.float32),
                precision=lax.Precision.HIGHEST,
            )
        )
    later_tokens = lax.optimization_barrier((tokens, *payloads))[0]
    shared = shared_expert(later_tokens, shared_weights)
    routed = jnp.stack(routed_steps)
    return (shared + routed).astype(jnp.bfloat16)


def solution(mesh):
    placed = (
        P(None, "ep", None),
        P(None, "ep", None),
        P(None, "ep", None),
        P("ep", None, None),
        P("ep", None, None),
        P("ep", None, None),
        P(None, None, "ep"),
    )
    return jax.shard_map(
        shards, mesh=mesh, in_specs=placed, out_specs=P(None, "ep", None), check_vma=False
    )
```

```python
import jax
import jax.numpy as jnp
from jax import lax
from jax.sharding import PartitionSpec as P
from jax.experimental import pallas as pl
from jax.experimental.pallas import tpu as pltpu


def partner_2(block, axis, apart):
    count = lax.axis_size(axis)
    route = []
    for low in range(count):
        high = low | 1 << apart
        if high != low and high < count:
            route += [(low, high), (high, low)]
    return lax.ppermute(block, axis, route)


def ffn_kernel(x_ref, gate_ref, up_ref, down_ref, out_ref, total):
    step = pl.program_id(0)

    @pl.when(step == 0)
    def _():
        total[...] = jnp.zeros_like(total)

    rows = x_ref[...].reshape(-1, x_ref.shape[-1])
    gate_val = jnp.dot(rows, gate_ref[...], preferred_element_type=jnp.float32)
    up_val = jnp.dot(rows, up_ref[...], preferred_element_type=jnp.float32)
    hidden = (gate_val / (1.0 + jnp.exp(-gate_val)) * up_val).astype(jnp.bfloat16)
    total[...] += jnp.dot(hidden, down_ref[...], preferred_element_type=jnp.float32)

    @pl.when(step == pl.num_programs(0) - 1)
    def _():
        out_ref[...] = total[...].astype(out_ref.dtype).reshape(out_ref.shape)


def expert_rows(token_block, w_gate, w_up, w_down, tile=256):
    model_width = token_block.shape[-1]
    row_count = token_block.size // model_width
    hidden_width = w_gate.shape[2]
    steps = hidden_width // tile
    flops = 6 * row_count * model_width * hidden_width
    weight_bytes = 3 * model_width * hidden_width * 2
    whole = (0,) * token_block.ndim
    return pl.pallas_call(
        ffn_kernel,
        out_shape=jax.ShapeDtypeStruct(token_block.shape, jnp.bfloat16),
        grid=(steps,),
        in_specs=[
            pl.BlockSpec(token_block.shape, lambda f: whole),
            pl.BlockSpec((None, model_width, tile), lambda f: (0, 0, f)),
            pl.BlockSpec((None, model_width, tile), lambda f: (0, 0, f)),
            pl.BlockSpec((None, tile, model_width), lambda f: (0, f, 0)),
        ],
        out_specs=pl.BlockSpec(token_block.shape, lambda f: whole),
        scratch_shapes=[pltpu.VMEM((row_count, model_width), jnp.float32)],
        compiler_params=pltpu.CompilerParams(
            dimension_semantics=("arbitrary",), vmem_limit_bytes=60 * 1024 * 1024
        ),
        cost_estimate=pl.CostEstimate(
            flops=flops,
            transcendentals=row_count * hidden_width,
            bytes_accessed=weight_bytes + 4 * row_count * model_width,
        ),
    )(token_block, w_gate, w_up, w_down)


def dispatch_kernel(select_ref, token_ref, out_ref):
    picked = jnp.dot(select_ref[...], token_ref[...], preferred_element_type=jnp.float32)
    out_ref[...] = picked.astype(out_ref.dtype).reshape(out_ref.shape)


def dispatch_rows(select, step_tokens, experts, capacity):
    model_width = step_tokens.shape[-1]
    return pl.pallas_call(
        dispatch_kernel,
        out_shape=jax.ShapeDtypeStruct((experts, capacity, model_width), step_tokens.dtype),
        in_specs=[
            pl.BlockSpec(memory_space=pltpu.VMEM),
            pl.BlockSpec(memory_space=pltpu.VMEM),
        ],
        out_specs=pl.BlockSpec(memory_space=pltpu.VMEM),
    )(select, step_tokens)


def route_tables(step_ids, step_weights, experts, capacity):
    row_count, top_count = step_ids.shape
    pair_count = row_count * top_count
    flat_ids = step_ids.reshape(pair_count)
    onehot = (flat_ids[:, None] == jnp.arange(experts, dtype=jnp.int32)[None, :]).astype(
        jnp.float32
    )
    earlier = (jnp.arange(pair_count)[:, None] > jnp.arange(pair_count)[None, :]).astype(
        jnp.float32
    )
    counts = jnp.dot(earlier, onehot, precision=lax.Precision.HIGHEST)
    slot_index = jnp.sum(counts * onehot, axis=1).astype(jnp.int32)
    position = flat_ids * capacity + slot_index
    placing = (
        position[:, None] == jnp.arange(experts * capacity, dtype=jnp.int32)[None, :]
    ).astype(jnp.float32)
    owner = (
        (jnp.arange(pair_count) // top_count)[:, None] == jnp.arange(row_count)[None, :]
    ).astype(jnp.float32)
    dispatch = jnp.dot(placing.T, owner, precision=lax.Precision.HIGHEST).astype(jnp.bfloat16)
    combine = jnp.dot(
        (owner * step_weights.reshape(pair_count)[:, None]).T,
        placing,
        precision=lax.Precision.HIGHEST,
    )
    return (dispatch, combine)


def join_halves(mine, partner, upper_side, axis_no):
    return jnp.where(
        upper_side,
        jnp.concatenate([partner, mine], axis=axis_no),
        jnp.concatenate([mine, partner], axis=axis_no),
    )


def shared_expert(tokens, shared_weights):
    my_index = lax.axis_index("ep")
    step_count, row_count, model_width = tokens.shape
    gathered = tokens
    for level in (2, 1, 0):
        partner = partner_2(gathered, "ep", level)
        gathered = join_halves(gathered, partner, my_index >> level & 1 == 1, 1)
    flat_rows = gathered.reshape(-1, model_width)
    gate_val = jnp.dot(flat_rows, shared_weights[0], preferred_element_type=jnp.float32)
    up_val = jnp.dot(flat_rows, shared_weights[1], preferred_element_type=jnp.float32)
    hidden = (jax.nn.silu(gate_val) * up_val).astype(jnp.bfloat16)
    partial_value = lax.dot_general(
        hidden, shared_weights[2], (((1,), (1,)), ((), ())), preferred_element_type=jnp.float32
    )
    partial_value = partial_value.reshape(step_count, 8 * row_count, model_width)
    for level in (0, 1, 2):
        half = partial_value.shape[1] // 2
        bit = my_index >> level & 1
        keep = lax.dynamic_slice_in_dim(partial_value, bit * half, half, 1)
        send = lax.dynamic_slice_in_dim(partial_value, (1 - bit) * half, half, 1)
        partial_value = keep + partner_2(send, "ep", level)
    return partial_value


def shards(tokens, expert_ids, combine_weights, w_gate, w_up, w_down, shared_weights):
    step_count, row_count, model_width = tokens.shape
    top_count = expert_ids.shape[2]
    device_count = lax.axis_size("ep")
    experts = w_gate.shape[0] * device_count
    capacity = max(2, row_count * top_count * 2 // experts)
    payloads = []
    combines = []
    for s in range(step_count):
        dispatch, combine = route_tables(expert_ids[s], combine_weights[s], experts, capacity)
        payloads.append(dispatch_rows(dispatch, tokens[s], experts, capacity))
        combines.append(combine)
    later_tokens = lax.optimization_barrier((tokens, *payloads))[0]
    shared = shared_expert(later_tokens, shared_weights)
    routed_steps = []
    for s in range(step_count):
        received = lax.all_to_all(payloads[s], "ep", split_axis=0, concat_axis=0, tiled=True)
        expert_out = expert_rows(received, w_gate, w_up, w_down)
        if s == 0:
            expert_out, shared = lax.optimization_barrier((expert_out, shared))
        returned = lax.all_to_all(expert_out, "ep", split_axis=0, concat_axis=0, tiled=True)
        routed_steps.append(
            jnp.einsum(
                "tec,ecd->td",
                combines[s].reshape(row_count, experts, capacity),
                returned.astype(jnp.float32),
                precision=lax.Precision.HIGHEST,
            )
        )
    routed = jnp.stack(routed_steps)
    return (shared + routed).astype(jnp.bfloat16)


def solution(mesh):
    placed = (
        P(None, "ep", None),
        P(None, "ep", None),
        P(None, "ep", None),
        P("ep", None, None),
        P("ep", None, None),
        P("ep", None, None),
        P(None, None, "ep"),
    )
    return jax.shard_map(
        shards, mesh=mesh, in_specs=placed, out_specs=P(None, "ep", None), check_vma=False
    )
```

```python
import jax
import jax.numpy as jnp
from jax import lax
from jax.sharding import PartitionSpec as P
from jax.experimental import pallas as pl
from jax.experimental.pallas import tpu as pltpu


def partner_2(block, axis, apart):
    count = lax.axis_size(axis)
    route = []
    for low in range(count):
        high = low | 1 << apart
        if high != low and high < count:
            route += [(low, high), (high, low)]
    return lax.ppermute(block, axis, route)


def ffn_kernel(x_ref, gate_ref, up_ref, down_ref, out_ref, total):
    step = pl.program_id(0)

    @pl.when(step == 0)
    def _():
        total[...] = jnp.zeros_like(total)

    rows = x_ref[...].reshape(-1, x_ref.shape[-1])
    gate_val = jnp.dot(rows, gate_ref[...], preferred_element_type=jnp.float32)
    up_val = jnp.dot(rows, up_ref[...], preferred_element_type=jnp.float32)
    hidden = (gate_val / (1.0 + jnp.exp(-gate_val)) * up_val).astype(jnp.bfloat16)
    total[...] += jnp.dot(hidden, down_ref[...], preferred_element_type=jnp.float32)

    @pl.when(step == pl.num_programs(0) - 1)
    def _():
        out_ref[...] = total[...].astype(out_ref.dtype).reshape(out_ref.shape)


def expert_rows(token_block, w_gate, w_up, w_down, tile=256):
    model_width = token_block.shape[-1]
    row_count = token_block.size // model_width
    hidden_width = w_gate.shape[2]
    steps = hidden_width // tile
    flops = 6 * row_count * model_width * hidden_width
    weight_bytes = 3 * model_width * hidden_width * 2
    whole = (0,) * token_block.ndim
    return pl.pallas_call(
        ffn_kernel,
        out_shape=jax.ShapeDtypeStruct(token_block.shape, jnp.bfloat16),
        grid=(steps,),
        in_specs=[
            pl.BlockSpec(token_block.shape, lambda f: whole),
            pl.BlockSpec((None, model_width, tile), lambda f: (0, 0, f)),
            pl.BlockSpec((None, model_width, tile), lambda f: (0, 0, f)),
            pl.BlockSpec((None, tile, model_width), lambda f: (0, f, 0)),
        ],
        out_specs=pl.BlockSpec(token_block.shape, lambda f: whole),
        scratch_shapes=[pltpu.VMEM((row_count, model_width), jnp.float32)],
        compiler_params=pltpu.CompilerParams(
            dimension_semantics=("arbitrary",), vmem_limit_bytes=60 * 1024 * 1024
        ),
        cost_estimate=pl.CostEstimate(
            flops=flops,
            transcendentals=row_count * hidden_width,
            bytes_accessed=weight_bytes + 4 * row_count * model_width,
        ),
    )(token_block, w_gate, w_up, w_down)


def dispatch_kernel(select_ref, token_ref, out_ref):
    picked = jnp.dot(select_ref[...], token_ref[...], preferred_element_type=jnp.float32)
    out_ref[...] = picked.astype(out_ref.dtype).reshape(out_ref.shape)


def dispatch_rows(select, step_tokens, experts, capacity):
    model_width = step_tokens.shape[-1]
    return pl.pallas_call(
        dispatch_kernel,
        out_shape=jax.ShapeDtypeStruct((experts, capacity, model_width), step_tokens.dtype),
        in_specs=[
            pl.BlockSpec(memory_space=pltpu.VMEM),
            pl.BlockSpec(memory_space=pltpu.VMEM),
        ],
        out_specs=pl.BlockSpec(memory_space=pltpu.VMEM),
    )(select, step_tokens)


def route_tables(step_ids, step_weights, experts, capacity):
    row_count, top_count = step_ids.shape
    pair_count = row_count * top_count
    flat_ids = step_ids.reshape(pair_count)
    onehot = (flat_ids[:, None] == jnp.arange(experts, dtype=jnp.int32)[None, :]).astype(
        jnp.float32
    )
    earlier = (jnp.arange(pair_count)[:, None] > jnp.arange(pair_count)[None, :]).astype(
        jnp.float32
    )
    counts = jnp.dot(earlier, onehot, precision=lax.Precision.HIGHEST)
    slot_index = jnp.sum(counts * onehot, axis=1).astype(jnp.int32)
    position = flat_ids * capacity + slot_index
    placing = (
        position[:, None] == jnp.arange(experts * capacity, dtype=jnp.int32)[None, :]
    ).astype(jnp.float32)
    owner = (
        (jnp.arange(pair_count) // top_count)[:, None] == jnp.arange(row_count)[None, :]
    ).astype(jnp.float32)
    dispatch = jnp.dot(placing.T, owner, precision=lax.Precision.HIGHEST).astype(jnp.bfloat16)
    combine = jnp.dot(
        (owner * step_weights.reshape(pair_count)[:, None]).T,
        placing,
        precision=lax.Precision.HIGHEST,
    )
    return (dispatch, combine)


def join_halves(mine, partner, upper_side, axis_no):
    return jnp.where(
        upper_side,
        jnp.concatenate([partner, mine], axis=axis_no),
        jnp.concatenate([mine, partner], axis=axis_no),
    )


def ring_shift(block, direction, ring):
    count = lax.axis_size("ep")
    route = []
    for low in range(count):
        place = low // 2 % ring
        route.append((low, low + ((place + direction) % ring - place) * 2))
    return lax.ppermute(block, "ep", route)


def shared_expert(tokens, shared_weights, ring=4):
    my_index = lax.axis_index("ep")
    step_count, row_count, model_width = tokens.shape
    gathered = tokens
    for level in (2, 1, 0):
        partner = partner_2(gathered, "ep", level)
        gathered = join_halves(gathered, partner, my_index >> level & 1 == 1, 1)
    flat_rows = gathered.reshape(-1, model_width)
    gate_val = jnp.dot(flat_rows, shared_weights[0], preferred_element_type=jnp.float32)
    up_val = jnp.dot(flat_rows, shared_weights[1], preferred_element_type=jnp.float32)
    hidden = (jax.nn.silu(gate_val) * up_val).astype(jnp.bfloat16)
    partial_value = lax.dot_general(
        hidden, shared_weights[2], (((1,), (1,)), ((), ())), preferred_element_type=jnp.float32
    )
    partial_value = partial_value.reshape(step_count, 8 * row_count, model_width)
    half = partial_value.shape[1] // 2
    bit = my_index & 1
    keep = lax.dynamic_slice_in_dim(partial_value, bit * half, half, 1)
    send = lax.dynamic_slice_in_dim(partial_value, (1 - bit) * half, half, 1)
    partial_value = keep + partner_2(send, "ep", 0)
    chunks = partial_value.reshape(step_count, ring, row_count, model_width)
    place = my_index // 2 % ring

    def chunk(s, target):
        slot = target % 2 * 2 + target // 2
        return lax.dynamic_index_in_dim(chunks[s], slot, 0, keepdims=False)

    results = []
    for s, direction in ((0, 1), (1, -1)):
        total = chunk(s, (place - direction) % ring)
        for k in range(ring - 1):
            arrived = ring_shift(total, direction, ring)
            total = arrived + chunk(s, (place - direction * (k + 2)) % ring)
        results.append(total)
    return jnp.stack(results)


def shards(tokens, expert_ids, combine_weights, w_gate, w_up, w_down, shared_weights):
    step_count, row_count, model_width = tokens.shape
    top_count = expert_ids.shape[2]
    device_count = lax.axis_size("ep")
    experts = w_gate.shape[0] * device_count
    capacity = max(2, row_count * top_count * 2 // experts)
    payloads = []
    combines = []
    for s in range(step_count):
        dispatch, combine = route_tables(expert_ids[s], combine_weights[s], experts, capacity)
        payloads.append(dispatch_rows(dispatch, tokens[s], experts, capacity))
        combines.append(combine)
    routed_steps = []
    for s in range(step_count):
        received = lax.all_to_all(payloads[s], "ep", split_axis=0, concat_axis=0, tiled=True)
        expert_out = expert_rows(received, w_gate, w_up, w_down)
        returned = lax.all_to_all(expert_out, "ep", split_axis=0, concat_axis=0, tiled=True)
        routed_steps.append(
            jnp.einsum(
                "tec,ecd->td",
                combines[s].reshape(row_count, experts, capacity),
                returned.astype(jnp.float32),
                precision=lax.Precision.HIGHEST,
            )
        )
    later_tokens = lax.optimization_barrier((tokens, *payloads))[0]
    shared = shared_expert(later_tokens, shared_weights)
    routed = jnp.stack(routed_steps)
    return (shared + routed).astype(jnp.bfloat16)


def solution(mesh):
    placed = (
        P(None, "ep", None),
        P(None, "ep", None),
        P(None, "ep", None),
        P("ep", None, None),
        P("ep", None, None),
        P("ep", None, None),
        P(None, None, "ep"),
    )
    return jax.shard_map(
        shards, mesh=mesh, in_specs=placed, out_specs=P(None, "ep", None), check_vma=False
    )
```

```python
import jax
import jax.numpy as jnp
from jax import lax
from jax.sharding import PartitionSpec as P
from jax.experimental import pallas as pl
from jax.experimental.pallas import tpu as pltpu


def partner_2(block, axis, apart):
    count = lax.axis_size(axis)
    route = []
    for low in range(count):
        high = low | 1 << apart
        if high != low and high < count:
            route += [(low, high), (high, low)]
    return lax.ppermute(block, axis, route)


def ffn_kernel(x_ref, gate_ref, up_ref, down_ref, out_ref, total):
    step = pl.program_id(0)

    @pl.when(step == 0)
    def _():
        total[...] = jnp.zeros_like(total)

    rows = x_ref[...].reshape(-1, x_ref.shape[-1])
    gate_val = jnp.dot(rows, gate_ref[...], preferred_element_type=jnp.float32)
    up_val = jnp.dot(rows, up_ref[...], preferred_element_type=jnp.float32)
    hidden = (gate_val / (1.0 + jnp.exp(-gate_val)) * up_val).astype(jnp.bfloat16)
    total[...] += jnp.dot(hidden, down_ref[...], preferred_element_type=jnp.float32)

    @pl.when(step == pl.num_programs(0) - 1)
    def _():
        out_ref[...] = total[...].astype(out_ref.dtype).reshape(out_ref.shape)


def expert_rows(token_block, w_gate, w_up, w_down, tile=256):
    model_width = token_block.shape[-1]
    row_count = token_block.size // model_width
    hidden_width = w_gate.shape[2]
    steps = hidden_width // tile
    flops = 6 * row_count * model_width * hidden_width
    weight_bytes = 3 * model_width * hidden_width * 2
    whole = (0,) * token_block.ndim
    return pl.pallas_call(
        ffn_kernel,
        out_shape=jax.ShapeDtypeStruct(token_block.shape, jnp.bfloat16),
        grid=(steps,),
        in_specs=[
            pl.BlockSpec(token_block.shape, lambda f: whole),
            pl.BlockSpec((None, model_width, tile), lambda f: (0, 0, f)),
            pl.BlockSpec((None, model_width, tile), lambda f: (0, 0, f)),
            pl.BlockSpec((None, tile, model_width), lambda f: (0, f, 0)),
        ],
        out_specs=pl.BlockSpec(token_block.shape, lambda f: whole),
        scratch_shapes=[pltpu.VMEM((row_count, model_width), jnp.float32)],
        compiler_params=pltpu.CompilerParams(
            dimension_semantics=("arbitrary",), vmem_limit_bytes=60 * 1024 * 1024
        ),
        cost_estimate=pl.CostEstimate(
            flops=flops,
            transcendentals=row_count * hidden_width,
            bytes_accessed=weight_bytes + 4 * row_count * model_width,
        ),
    )(token_block, w_gate, w_up, w_down)


def dispatch_kernel(select_ref, token_ref, out_ref):
    picked = jnp.dot(select_ref[...], token_ref[...], preferred_element_type=jnp.float32)
    out_ref[...] = picked.astype(out_ref.dtype).reshape(out_ref.shape)


def dispatch_rows(select, step_tokens, experts, capacity):
    model_width = step_tokens.shape[-1]
    return pl.pallas_call(
        dispatch_kernel,
        out_shape=jax.ShapeDtypeStruct((experts, capacity, model_width), step_tokens.dtype),
        in_specs=[
            pl.BlockSpec(memory_space=pltpu.VMEM),
            pl.BlockSpec(memory_space=pltpu.VMEM),
        ],
        out_specs=pl.BlockSpec(memory_space=pltpu.VMEM),
    )(select, step_tokens)


def route_tables(step_ids, step_weights, experts, capacity):
    row_count, top_count = step_ids.shape
    pair_count = row_count * top_count
    flat_ids = step_ids.reshape(pair_count)
    onehot = (flat_ids[:, None] == jnp.arange(experts, dtype=jnp.int32)[None, :]).astype(
        jnp.float32
    )
    earlier = (jnp.arange(pair_count)[:, None] > jnp.arange(pair_count)[None, :]).astype(
        jnp.float32
    )
    counts = jnp.dot(earlier, onehot, precision=lax.Precision.HIGHEST)
    slot_index = jnp.sum(counts * onehot, axis=1).astype(jnp.int32)
    position = flat_ids * capacity + slot_index
    placing = (
        position[:, None] == jnp.arange(experts * capacity, dtype=jnp.int32)[None, :]
    ).astype(jnp.float32)
    owner = (
        (jnp.arange(pair_count) // top_count)[:, None] == jnp.arange(row_count)[None, :]
    ).astype(jnp.float32)
    dispatch = jnp.dot(placing.T, owner, precision=lax.Precision.HIGHEST).astype(jnp.bfloat16)
    combine = jnp.dot(
        (owner * step_weights.reshape(pair_count)[:, None]).T,
        placing,
        precision=lax.Precision.HIGHEST,
    )
    return (dispatch, combine)


def join_halves(mine, partner, upper_side, axis_no):
    return jnp.where(
        upper_side,
        jnp.concatenate([partner, mine], axis=axis_no),
        jnp.concatenate([mine, partner], axis=axis_no),
    )


def ring_shift(block, direction, ring):
    count = lax.axis_size("ep")
    route = []
    for low in range(count):
        place = low // 2 % ring
        route.append((low, low + ((place + direction) % ring - place) * 2))
    return lax.ppermute(block, "ep", route)


def shared_expert(tokens, shared_weights, ring=4):
    my_index = lax.axis_index("ep")
    step_count, row_count, model_width = tokens.shape
    gathered = tokens
    for level in (2, 1, 0):
        partner = partner_2(gathered, "ep", level)
        gathered = join_halves(gathered, partner, my_index >> level & 1 == 1, 1)
    flat_rows = gathered.reshape(-1, model_width)
    gate_val = jnp.dot(flat_rows, shared_weights[0], preferred_element_type=jnp.float32)
    up_val = jnp.dot(flat_rows, shared_weights[1], preferred_element_type=jnp.float32)
    hidden = (jax.nn.silu(gate_val) * up_val).astype(jnp.bfloat16)
    partial_value = lax.dot_general(
        hidden, shared_weights[2], (((1,), (1,)), ((), ())), preferred_element_type=jnp.float32
    )
    partial_value = partial_value.reshape(step_count, 8 * row_count, model_width)
    half = partial_value.shape[1] // 2
    bit = my_index & 1
    keep = lax.dynamic_slice_in_dim(partial_value, bit * half, half, 1)
    send = lax.dynamic_slice_in_dim(partial_value, (1 - bit) * half, half, 1)
    partial_value = keep + partner_2(send, "ep", 0)
    chunks = partial_value.reshape(step_count, ring, row_count, model_width)
    place = my_index // 2 % ring

    def chunk(s, target):
        slot = target % 2 * 2 + target // 2
        return lax.dynamic_index_in_dim(chunks[s], slot, 0, keepdims=False)

    results = []
    for s, direction in ((0, 1), (1, -1)):
        total = chunk(s, (place - direction) % ring)
        for k in range(ring - 1):
            arrived = ring_shift(total, direction, ring)
            total = arrived + chunk(s, (place - direction * (k + 2)) % ring)
        results.append(total)
    return jnp.stack(results)


def shards(tokens, expert_ids, combine_weights, w_gate, w_up, w_down, shared_weights):
    step_count, row_count, model_width = tokens.shape
    top_count = expert_ids.shape[2]
    device_count = lax.axis_size("ep")
    experts = w_gate.shape[0] * device_count
    capacity = max(2, row_count * top_count * 2 // experts)
    payloads = []
    combines = []
    for s in range(step_count):
        dispatch, combine = route_tables(expert_ids[s], combine_weights[s], experts, capacity)
        payloads.append(dispatch_rows(dispatch, tokens[s], experts, capacity))
        combines.append(combine)
    later_tokens = lax.optimization_barrier((tokens, *payloads))[0]
    shared = shared_expert(later_tokens, shared_weights)
    routed_steps = []
    for s in range(step_count):
        received = lax.all_to_all(payloads[s], "ep", split_axis=0, concat_axis=0, tiled=True)
        if s == step_count - 1:
            received, shared = lax.optimization_barrier((received, shared))
        expert_out = expert_rows(received, w_gate, w_up, w_down)
        returned = lax.all_to_all(expert_out, "ep", split_axis=0, concat_axis=0, tiled=True)
        routed_steps.append(
            jnp.einsum(
                "tec,ecd->td",
                combines[s].reshape(row_count, experts, capacity),
                returned.astype(jnp.float32),
                precision=lax.Precision.HIGHEST,
            )
        )
    routed = jnp.stack(routed_steps)
    return (shared + routed).astype(jnp.bfloat16)


def solution(mesh):
    placed = (
        P(None, "ep", None),
        P(None, "ep", None),
        P(None, "ep", None),
        P("ep", None, None),
        P("ep", None, None),
        P("ep", None, None),
        P(None, None, "ep"),
    )
    return jax.shard_map(
        shards, mesh=mesh, in_specs=placed, out_specs=P(None, "ep", None), check_vma=False
    )
```

```python
import jax
import jax.numpy as jnp
from jax import lax
from jax.sharding import PartitionSpec as P
from jax.experimental import pallas as pl
from jax.experimental.pallas import tpu as pltpu


def partner_2(block, axis, apart):
    count = lax.axis_size(axis)
    route = []
    for low in range(count):
        high = low | 1 << apart
        if high != low and high < count:
            route += [(low, high), (high, low)]
    return lax.ppermute(block, axis, route)


def ffn_kernel(x_ref, gate_ref, up_ref, down_ref, out_ref, total):
    step = pl.program_id(0)

    @pl.when(step == 0)
    def _():
        total[...] = jnp.zeros_like(total)

    rows = x_ref[...].reshape(-1, x_ref.shape[-1])
    gate_val = jnp.dot(rows, gate_ref[...], preferred_element_type=jnp.float32)
    up_val = jnp.dot(rows, up_ref[...], preferred_element_type=jnp.float32)
    hidden = (gate_val / (1.0 + jnp.exp(-gate_val)) * up_val).astype(jnp.bfloat16)
    total[...] += jnp.dot(hidden, down_ref[...], preferred_element_type=jnp.float32)

    @pl.when(step == pl.num_programs(0) - 1)
    def _():
        out_ref[...] = total[...].astype(out_ref.dtype).reshape(out_ref.shape)


def expert_rows(token_block, w_gate, w_up, w_down, tile=256):
    model_width = token_block.shape[-1]
    row_count = token_block.size // model_width
    hidden_width = w_gate.shape[2]
    steps = hidden_width // tile
    flops = 6 * row_count * model_width * hidden_width
    weight_bytes = 3 * model_width * hidden_width * 2
    whole = (0,) * token_block.ndim
    return pl.pallas_call(
        ffn_kernel,
        out_shape=jax.ShapeDtypeStruct(token_block.shape, jnp.bfloat16),
        grid=(steps,),
        in_specs=[
            pl.BlockSpec(token_block.shape, lambda f: whole),
            pl.BlockSpec((None, model_width, tile), lambda f: (0, 0, f)),
            pl.BlockSpec((None, model_width, tile), lambda f: (0, 0, f)),
            pl.BlockSpec((None, tile, model_width), lambda f: (0, f, 0)),
        ],
        out_specs=pl.BlockSpec(token_block.shape, lambda f: whole),
        scratch_shapes=[pltpu.VMEM((row_count, model_width), jnp.float32)],
        compiler_params=pltpu.CompilerParams(
            dimension_semantics=("arbitrary",), vmem_limit_bytes=60 * 1024 * 1024
        ),
        cost_estimate=pl.CostEstimate(
            flops=flops,
            transcendentals=row_count * hidden_width,
            bytes_accessed=weight_bytes + 4 * row_count * model_width,
        ),
    )(token_block, w_gate, w_up, w_down)


def route_tables(step_ids, step_weights, experts, capacity):
    row_count, top_count = step_ids.shape
    pair_count = row_count * top_count
    flat_ids = step_ids.reshape(pair_count)
    onehot = (flat_ids[:, None] == jnp.arange(experts, dtype=jnp.int32)[None, :]).astype(
        jnp.float32
    )
    earlier = (jnp.arange(pair_count)[:, None] > jnp.arange(pair_count)[None, :]).astype(
        jnp.float32
    )
    counts = jnp.dot(earlier, onehot, precision=lax.Precision.HIGHEST)
    slot_index = jnp.sum(counts * onehot, axis=1).astype(jnp.int32)
    position = flat_ids * capacity + slot_index
    placing = (
        position[:, None] == jnp.arange(experts * capacity, dtype=jnp.int32)[None, :]
    ).astype(jnp.float32)
    owner = (
        (jnp.arange(pair_count) // top_count)[:, None] == jnp.arange(row_count)[None, :]
    ).astype(jnp.float32)
    dispatch = jnp.dot(placing.T, owner, precision=lax.Precision.HIGHEST).astype(jnp.bfloat16)
    combine = jnp.dot(
        (owner * step_weights.reshape(pair_count)[:, None]).T,
        placing,
        precision=lax.Precision.HIGHEST,
    )
    return (dispatch, combine)


def join_halves(mine, partner, upper_side, axis_no):
    return jnp.where(
        upper_side,
        jnp.concatenate([partner, mine], axis=axis_no),
        jnp.concatenate([mine, partner], axis=axis_no),
    )


def shared_expert(tokens, shared_weights, after):
    step_count, row_count, model_width = tokens.shape
    count = lax.axis_size("ep")
    groups = [list(range(g, g + 8)) for g in range(0, count, 8)]
    gathered = lax.all_gather(tokens, "ep", axis=1, tiled=True, axis_index_groups=groups)
    gathered = lax.optimization_barrier((gathered, after))[0]
    flat_rows = gathered.reshape(-1, model_width)
    gate_val = jnp.dot(flat_rows, shared_weights[0], preferred_element_type=jnp.float32)
    up_val = jnp.dot(flat_rows, shared_weights[1], preferred_element_type=jnp.float32)
    hidden = (jax.nn.silu(gate_val) * up_val).astype(jnp.bfloat16)
    partial_value = lax.dot_general(
        hidden, shared_weights[2], (((1,), (1,)), ((), ())), preferred_element_type=jnp.float32
    )
    partial_value = partial_value.reshape(step_count, 8 * row_count, model_width)
    return lax.psum_scatter(
        partial_value, "ep", scatter_dimension=1, tiled=True, axis_index_groups=groups
    )


def shards(tokens, expert_ids, combine_weights, w_gate, w_up, w_down, shared_weights):
    step_count, row_count, model_width = tokens.shape
    top_count = expert_ids.shape[2]
    device_count = lax.axis_size("ep")
    experts = w_gate.shape[0] * device_count
    capacity = max(2, row_count * top_count * 2 // experts)
    payloads = []
    combines = []
    for s in range(step_count):
        dispatch, combine = route_tables(expert_ids[s], combine_weights[s], experts, capacity)
        payloads.append(
            jnp.einsum(
                "ect,td->ecd",
                dispatch.reshape(experts, capacity, row_count),
                tokens[s],
                preferred_element_type=jnp.float32,
            ).astype(jnp.bfloat16)
        )
        combines.append(combine)
    routed_steps = []
    arrived = []
    for s in range(step_count):
        received = lax.all_to_all(payloads[s], "ep", split_axis=0, concat_axis=0, tiled=True)
        arrived.append(received)
        expert_out = expert_rows(received, w_gate, w_up, w_down)
        returned = lax.all_to_all(expert_out, "ep", split_axis=0, concat_axis=0, tiled=True)
        routed_steps.append(
            jnp.einsum(
                "tec,ecd->td",
                combines[s].reshape(row_count, experts, capacity),
                returned.astype(jnp.float32),
                precision=lax.Precision.HIGHEST,
            )
        )
    shared = shared_expert(tokens, shared_weights, arrived[0])
    routed = jnp.stack(routed_steps)
    return (shared + routed).astype(jnp.bfloat16)


def solution(mesh):
    placed = (
        P(None, "ep", None),
        P(None, "ep", None),
        P(None, "ep", None),
        P("ep", None, None),
        P("ep", None, None),
        P("ep", None, None),
        P(None, None, "ep"),
    )
    return jax.shard_map(
        shards, mesh=mesh, in_specs=placed, out_specs=P(None, "ep", None), check_vma=False
    )
```

```python
import jax
import jax.numpy as jnp
from jax import lax
from jax.sharding import PartitionSpec as P
from jax.experimental import pallas as pl
from jax.experimental.pallas import tpu as pltpu


def partner_2(block, axis, apart):
    count = lax.axis_size(axis)
    route = []
    for low in range(count):
        high = low | 1 << apart
        if high != low and high < count:
            route += [(low, high), (high, low)]
    return lax.ppermute(block, axis, route)


def ffn_kernel(x_ref, gate_ref, up_ref, down_ref, out_ref, total):
    step = pl.program_id(0)

    @pl.when(step == 0)
    def _():
        total[...] = jnp.zeros_like(total)

    rows = x_ref[...].reshape(-1, x_ref.shape[-1])
    gate_val = jnp.dot(rows, gate_ref[...], preferred_element_type=jnp.float32)
    up_val = jnp.dot(rows, up_ref[...], preferred_element_type=jnp.float32)
    hidden = (gate_val / (1.0 + jnp.exp(-gate_val)) * up_val).astype(jnp.bfloat16)
    total[...] += jnp.dot(hidden, down_ref[...], preferred_element_type=jnp.float32)

    @pl.when(step == pl.num_programs(0) - 1)
    def _():
        out_ref[...] = total[...].astype(out_ref.dtype).reshape(out_ref.shape)


def expert_rows(token_block, w_gate, w_up, w_down, tile=256):
    model_width = token_block.shape[-1]
    row_count = token_block.size // model_width
    hidden_width = w_gate.shape[2]
    steps = hidden_width // tile
    flops = 6 * row_count * model_width * hidden_width
    weight_bytes = 3 * model_width * hidden_width * 2
    whole = (0,) * token_block.ndim
    return pl.pallas_call(
        ffn_kernel,
        out_shape=jax.ShapeDtypeStruct(token_block.shape, jnp.bfloat16),
        grid=(steps,),
        in_specs=[
            pl.BlockSpec(token_block.shape, lambda f: whole),
            pl.BlockSpec((None, model_width, tile), lambda f: (0, 0, f)),
            pl.BlockSpec((None, model_width, tile), lambda f: (0, 0, f)),
            pl.BlockSpec((None, tile, model_width), lambda f: (0, f, 0)),
        ],
        out_specs=pl.BlockSpec(token_block.shape, lambda f: whole),
        scratch_shapes=[pltpu.VMEM((row_count, model_width), jnp.float32)],
        compiler_params=pltpu.CompilerParams(
            dimension_semantics=("arbitrary",), vmem_limit_bytes=60 * 1024 * 1024
        ),
        cost_estimate=pl.CostEstimate(
            flops=flops,
            transcendentals=row_count * hidden_width,
            bytes_accessed=weight_bytes + 4 * row_count * model_width,
        ),
    )(token_block, w_gate, w_up, w_down)


def dispatch_kernel(select_ref, token_ref, out_ref):
    picked = jnp.dot(select_ref[...], token_ref[...], preferred_element_type=jnp.float32)
    out_ref[...] = picked.astype(out_ref.dtype).reshape(out_ref.shape)


def dispatch_rows(select, step_tokens, experts, capacity):
    model_width = step_tokens.shape[-1]
    return pl.pallas_call(
        dispatch_kernel,
        out_shape=jax.ShapeDtypeStruct((experts, capacity, model_width), step_tokens.dtype),
        in_specs=[
            pl.BlockSpec(memory_space=pltpu.VMEM),
            pl.BlockSpec(memory_space=pltpu.VMEM),
        ],
        out_specs=pl.BlockSpec(memory_space=pltpu.VMEM),
    )(select, step_tokens)


def route_tables(step_ids, step_weights, experts, capacity):
    row_count, top_count = step_ids.shape
    pair_count = row_count * top_count
    flat_ids = step_ids.reshape(pair_count)
    onehot = (flat_ids[:, None] == jnp.arange(experts, dtype=jnp.int32)[None, :]).astype(
        jnp.float32
    )
    earlier = (jnp.arange(pair_count)[:, None] > jnp.arange(pair_count)[None, :]).astype(
        jnp.float32
    )
    counts = jnp.dot(earlier, onehot, precision=lax.Precision.HIGHEST)
    slot_index = jnp.sum(counts * onehot, axis=1).astype(jnp.int32)
    position = flat_ids * capacity + slot_index
    placing = (
        position[:, None] == jnp.arange(experts * capacity, dtype=jnp.int32)[None, :]
    ).astype(jnp.float32)
    owner = (
        (jnp.arange(pair_count) // top_count)[:, None] == jnp.arange(row_count)[None, :]
    ).astype(jnp.float32)
    dispatch = jnp.dot(placing.T, owner, precision=lax.Precision.HIGHEST).astype(jnp.bfloat16)
    combine = jnp.dot(
        (owner * step_weights.reshape(pair_count)[:, None]).T,
        placing,
        precision=lax.Precision.HIGHEST,
    )
    return (dispatch, combine)


def join_halves(mine, partner, upper_side, axis_no):
    return jnp.where(
        upper_side,
        jnp.concatenate([partner, mine], axis=axis_no),
        jnp.concatenate([mine, partner], axis=axis_no),
    )


def ring_shift(block, direction, ring):
    count = lax.axis_size("ep")
    route = []
    for low in range(count):
        place = low // 2 % ring
        route.append((low, low + ((place + direction) % ring - place) * 2))
    return lax.ppermute(block, "ep", route)


def shared_expert(tokens, shared_weights, ring=4):
    my_index = lax.axis_index("ep")
    step_count, row_count, model_width = tokens.shape
    gathered = tokens
    for level in (2, 1, 0):
        partner = partner_2(gathered, "ep", level)
        gathered = join_halves(gathered, partner, my_index >> level & 1 == 1, 1)
    flat_rows = gathered.reshape(-1, model_width)
    gate_val = jnp.dot(flat_rows, shared_weights[0], preferred_element_type=jnp.float32)
    up_val = jnp.dot(flat_rows, shared_weights[1], preferred_element_type=jnp.float32)
    hidden = (jax.nn.silu(gate_val) * up_val).astype(jnp.bfloat16)
    partial_value = lax.dot_general(
        hidden, shared_weights[2], (((1,), (1,)), ((), ())), preferred_element_type=jnp.float32
    )
    partial_value = partial_value.reshape(step_count, 8 * row_count, model_width)
    half = partial_value.shape[1] // 2
    bit = my_index & 1
    keep = lax.dynamic_slice_in_dim(partial_value, bit * half, half, 1)
    send = lax.dynamic_slice_in_dim(partial_value, (1 - bit) * half, half, 1)
    partial_value = keep + partner_2(send, "ep", 0)
    chunks = partial_value.reshape(step_count, ring, row_count, model_width)
    place = my_index // 2 % ring

    def chunk(s, target):
        slot = target % 2 * 2 + target // 2
        return lax.dynamic_index_in_dim(chunks[s], slot, 0, keepdims=False)

    total = jnp.stack([chunk(s, place) for s in range(step_count)])
    for offset in range(1, ring):
        outgoing = jnp.stack([chunk(s, (place + offset) % ring) for s in range(step_count)])
        total = total + ring_shift(outgoing, offset, ring)
    return total


def shards(tokens, expert_ids, combine_weights, w_gate, w_up, w_down, shared_weights):
    step_count, row_count, model_width = tokens.shape
    top_count = expert_ids.shape[2]
    device_count = lax.axis_size("ep")
    experts = w_gate.shape[0] * device_count
    capacity = max(2, row_count * top_count * 2 // experts)
    payloads = []
    combines = []
    for s in range(step_count):
        dispatch, combine = route_tables(expert_ids[s], combine_weights[s], experts, capacity)
        payloads.append(dispatch_rows(dispatch, tokens[s], experts, capacity))
        combines.append(combine)
    routed_steps = []
    for s in range(step_count):
        received = lax.all_to_all(payloads[s], "ep", split_axis=0, concat_axis=0, tiled=True)
        expert_out = expert_rows(received, w_gate, w_up, w_down)
        returned = lax.all_to_all(expert_out, "ep", split_axis=0, concat_axis=0, tiled=True)
        routed_steps.append(
            jnp.einsum(
                "tec,ecd->td",
                combines[s].reshape(row_count, experts, capacity),
                returned.astype(jnp.float32),
                precision=lax.Precision.HIGHEST,
            )
        )
    later_tokens = lax.optimization_barrier((tokens, *payloads))[0]
    shared = shared_expert(later_tokens, shared_weights)
    routed = jnp.stack(routed_steps)
    return (shared + routed).astype(jnp.bfloat16)


def solution(mesh):
    placed = (
        P(None, "ep", None),
        P(None, "ep", None),
        P(None, "ep", None),
        P("ep", None, None),
        P("ep", None, None),
        P("ep", None, None),
        P(None, None, "ep"),
    )
    return jax.shard_map(
        shards, mesh=mesh, in_specs=placed, out_specs=P(None, "ep", None), check_vma=False
    )
```

```python
import jax
import jax.numpy as jnp
from jax import lax
from jax.sharding import PartitionSpec as P
from jax.experimental import pallas as pl
from jax.experimental.pallas import tpu as pltpu


def partner_2(block, axis, apart):
    count = lax.axis_size(axis)
    route = []
    for low in range(count):
        high = low | 1 << apart
        if high != low and high < count:
            route += [(low, high), (high, low)]
    return lax.ppermute(block, axis, route)


def ffn_kernel(x_ref, gate_ref, up_ref, down_ref, out_ref, total):
    step = pl.program_id(0)

    @pl.when(step == 0)
    def _():
        total[...] = jnp.zeros_like(total)

    rows = x_ref[...].reshape(-1, x_ref.shape[-1])
    gate_val = jnp.dot(rows, gate_ref[...], preferred_element_type=jnp.float32)
    up_val = jnp.dot(rows, up_ref[...], preferred_element_type=jnp.float32)
    hidden = (gate_val / (1.0 + jnp.exp(-gate_val)) * up_val).astype(jnp.bfloat16)
    total[...] += jnp.dot(hidden, down_ref[...], preferred_element_type=jnp.float32)

    @pl.when(step == pl.num_programs(0) - 1)
    def _():
        out_ref[...] = total[...].astype(out_ref.dtype).reshape(out_ref.shape)


def expert_rows(token_block, w_gate, w_up, w_down, tile=256):
    model_width = token_block.shape[-1]
    row_count = token_block.size // model_width
    hidden_width = w_gate.shape[2]
    steps = hidden_width // tile
    flops = 6 * row_count * model_width * hidden_width
    weight_bytes = 3 * model_width * hidden_width * 2
    whole = (0,) * token_block.ndim
    return pl.pallas_call(
        ffn_kernel,
        out_shape=jax.ShapeDtypeStruct(token_block.shape, jnp.bfloat16),
        grid=(steps,),
        in_specs=[
            pl.BlockSpec(token_block.shape, lambda f: whole),
            pl.BlockSpec((None, model_width, tile), lambda f: (0, 0, f)),
            pl.BlockSpec((None, model_width, tile), lambda f: (0, 0, f)),
            pl.BlockSpec((None, tile, model_width), lambda f: (0, f, 0)),
        ],
        out_specs=pl.BlockSpec(token_block.shape, lambda f: whole),
        scratch_shapes=[pltpu.VMEM((row_count, model_width), jnp.float32)],
        compiler_params=pltpu.CompilerParams(
            dimension_semantics=("arbitrary",), vmem_limit_bytes=60 * 1024 * 1024
        ),
        cost_estimate=pl.CostEstimate(
            flops=flops,
            transcendentals=row_count * hidden_width,
            bytes_accessed=weight_bytes + 4 * row_count * model_width,
        ),
    )(token_block, w_gate, w_up, w_down)


def dispatch_kernel(select_ref, token_ref, out_ref):
    picked = jnp.dot(select_ref[...], token_ref[...], preferred_element_type=jnp.float32)
    out_ref[...] = picked.astype(out_ref.dtype).reshape(out_ref.shape)


def dispatch_rows(select, step_tokens, experts, capacity):
    model_width = step_tokens.shape[-1]
    return pl.pallas_call(
        dispatch_kernel,
        out_shape=jax.ShapeDtypeStruct((experts, capacity, model_width), step_tokens.dtype),
        in_specs=[
            pl.BlockSpec(memory_space=pltpu.VMEM),
            pl.BlockSpec(memory_space=pltpu.VMEM),
        ],
        out_specs=pl.BlockSpec(memory_space=pltpu.VMEM),
    )(select, step_tokens)


def route_tables(step_ids, step_weights, experts, capacity):
    row_count, top_count = step_ids.shape
    pair_count = row_count * top_count
    flat_ids = step_ids.reshape(pair_count)
    onehot = (flat_ids[:, None] == jnp.arange(experts, dtype=jnp.int32)[None, :]).astype(
        jnp.float32
    )
    earlier = (jnp.arange(pair_count)[:, None] > jnp.arange(pair_count)[None, :]).astype(
        jnp.float32
    )
    counts = jnp.dot(earlier, onehot, precision=lax.Precision.HIGHEST)
    slot_index = jnp.sum(counts * onehot, axis=1).astype(jnp.int32)
    position = flat_ids * capacity + slot_index
    placing = (
        position[:, None] == jnp.arange(experts * capacity, dtype=jnp.int32)[None, :]
    ).astype(jnp.float32)
    owner = (
        (jnp.arange(pair_count) // top_count)[:, None] == jnp.arange(row_count)[None, :]
    ).astype(jnp.float32)
    dispatch = jnp.dot(placing.T, owner, precision=lax.Precision.HIGHEST).astype(jnp.bfloat16)
    combine = jnp.dot(
        (owner * step_weights.reshape(pair_count)[:, None]).T,
        placing,
        precision=lax.Precision.HIGHEST,
    )
    return (dispatch, combine)


def join_halves(mine, partner, upper_side, axis_no):
    return jnp.where(
        upper_side,
        jnp.concatenate([partner, mine], axis=axis_no),
        jnp.concatenate([mine, partner], axis=axis_no),
    )


def ring_shift(block, direction, ring):
    count = lax.axis_size("ep")
    route = []
    for low in range(count):
        place = low // 2 % ring
        route.append((low, low + ((place + direction) % ring - place) * 2))
    return lax.ppermute(block, "ep", route)


def shared_expert(tokens, shared_weights, ring=4):
    my_index = lax.axis_index("ep")
    step_count, row_count, model_width = tokens.shape
    gathered = tokens
    for level in (2, 1, 0):
        partner = partner_2(gathered, "ep", level)
        gathered = join_halves(gathered, partner, my_index >> level & 1 == 1, 1)
    flat_rows = gathered.reshape(-1, model_width)
    gate_val = jnp.dot(flat_rows, shared_weights[0], preferred_element_type=jnp.float32)
    up_val = jnp.dot(flat_rows, shared_weights[1], preferred_element_type=jnp.float32)
    hidden = (jax.nn.silu(gate_val) * up_val).astype(jnp.bfloat16)
    partial_value = lax.dot_general(
        hidden, shared_weights[2], (((1,), (1,)), ((), ())), preferred_element_type=jnp.float32
    )
    partial_value = partial_value.reshape(step_count, 8 * row_count, model_width)
    half = partial_value.shape[1] // 2
    bit = my_index & 1
    keep = lax.dynamic_slice_in_dim(partial_value, bit * half, half, 1)
    send = lax.dynamic_slice_in_dim(partial_value, (1 - bit) * half, half, 1)
    partial_value = keep + partner_2(send, "ep", 0)
    chunks = partial_value.reshape(step_count, ring, row_count, model_width)
    place = my_index // 2 % ring

    def chunk(s, target):
        slot = target % 2 * 2 + target // 2
        return lax.dynamic_index_in_dim(chunks[s], slot, 0, keepdims=False)

    results = []
    for s, direction in ((0, 1), (1, -1)):
        total = chunk(s, (place - direction) % ring)
        for k in range(ring - 1):
            arrived = ring_shift(total, direction, ring)
            total = arrived + chunk(s, (place - direction * (k + 2)) % ring)
        results.append(total)
    return jnp.stack(results)


def shards(tokens, expert_ids, combine_weights, w_gate, w_up, w_down, shared_weights):
    step_count, row_count, model_width = tokens.shape
    top_count = expert_ids.shape[2]
    device_count = lax.axis_size("ep")
    experts = w_gate.shape[0] * device_count
    capacity = max(2, row_count * top_count * 2 // experts)
    payloads = []
    combines = []
    for s in range(step_count):
        dispatch, combine = route_tables(expert_ids[s], combine_weights[s], experts, capacity)
        payloads.append(dispatch_rows(dispatch, tokens[s], experts, capacity))
        combines.append(combine)
    later_tokens = lax.optimization_barrier((tokens, *payloads))[0]
    shared = shared_expert(later_tokens, shared_weights)
    routed_steps = []
    for s in range(step_count):
        received = lax.all_to_all(payloads[s], "ep", split_axis=0, concat_axis=0, tiled=True)
        expert_out = expert_rows(received, w_gate, w_up, w_down)
        if s == step_count - 1:
            expert_out, shared = lax.optimization_barrier((expert_out, shared))
        returned = lax.all_to_all(expert_out, "ep", split_axis=0, concat_axis=0, tiled=True)
        routed_steps.append(
            jnp.einsum(
                "tec,ecd->td",
                combines[s].reshape(row_count, experts, capacity),
                returned.astype(jnp.float32),
                precision=lax.Precision.HIGHEST,
            )
        )
    routed = jnp.stack(routed_steps)
    return (shared + routed).astype(jnp.bfloat16)


def solution(mesh):
    placed = (
        P(None, "ep", None),
        P(None, "ep", None),
        P(None, "ep", None),
        P("ep", None, None),
        P("ep", None, None),
        P("ep", None, None),
        P(None, None, "ep"),
    )
    return jax.shard_map(
        shards, mesh=mesh, in_specs=placed, out_specs=P(None, "ep", None), check_vma=False
    )
```

```python
import jax
import jax.numpy as jnp
from jax import lax
from jax.sharding import PartitionSpec as P
from jax.experimental import pallas as pl
from jax.experimental.pallas import tpu as pltpu


def partner_2(block, axis, apart):
    count = lax.axis_size(axis)
    route = []
    for low in range(count):
        high = low | 1 << apart
        if high != low and high < count:
            route += [(low, high), (high, low)]
    return lax.ppermute(block, axis, route)


def ffn_kernel(x_ref, gate_ref, up_ref, down_ref, out_ref, total):
    step = pl.program_id(0)

    @pl.when(step == 0)
    def _():
        total[...] = jnp.zeros_like(total)

    rows = x_ref[...].reshape(-1, x_ref.shape[-1])
    gate_val = jnp.dot(rows, gate_ref[...], preferred_element_type=jnp.float32)
    up_val = jnp.dot(rows, up_ref[...], preferred_element_type=jnp.float32)
    hidden = (gate_val / (1.0 + jnp.exp(-gate_val)) * up_val).astype(jnp.bfloat16)
    total[...] += jnp.dot(hidden, down_ref[...], preferred_element_type=jnp.float32)

    @pl.when(step == pl.num_programs(0) - 1)
    def _():
        out_ref[...] = total[...].astype(out_ref.dtype).reshape(out_ref.shape)


def expert_rows(token_block, w_gate, w_up, w_down, tile=256):
    model_width = token_block.shape[-1]
    row_count = token_block.size // model_width
    hidden_width = w_gate.shape[2]
    steps = hidden_width // tile
    flops = 6 * row_count * model_width * hidden_width
    weight_bytes = 3 * model_width * hidden_width * 2
    whole = (0,) * token_block.ndim
    return pl.pallas_call(
        ffn_kernel,
        out_shape=jax.ShapeDtypeStruct(token_block.shape, jnp.bfloat16),
        grid=(steps,),
        in_specs=[
            pl.BlockSpec(token_block.shape, lambda f: whole),
            pl.BlockSpec((None, model_width, tile), lambda f: (0, 0, f)),
            pl.BlockSpec((None, model_width, tile), lambda f: (0, 0, f)),
            pl.BlockSpec((None, tile, model_width), lambda f: (0, f, 0)),
        ],
        out_specs=pl.BlockSpec(token_block.shape, lambda f: whole),
        scratch_shapes=[pltpu.VMEM((row_count, model_width), jnp.float32)],
        compiler_params=pltpu.CompilerParams(
            dimension_semantics=("arbitrary",), vmem_limit_bytes=60 * 1024 * 1024
        ),
        cost_estimate=pl.CostEstimate(
            flops=flops,
            transcendentals=row_count * hidden_width,
            bytes_accessed=weight_bytes + 4 * row_count * model_width,
        ),
    )(token_block, w_gate, w_up, w_down)


def dispatch_kernel(select_ref, token_ref, out_ref):
    picked = jnp.dot(select_ref[...], token_ref[...], preferred_element_type=jnp.float32)
    out_ref[...] = picked.astype(out_ref.dtype).reshape(out_ref.shape)


def dispatch_rows(select, step_tokens, experts, capacity):
    model_width = step_tokens.shape[-1]
    return pl.pallas_call(
        dispatch_kernel,
        out_shape=jax.ShapeDtypeStruct((experts, capacity, model_width), step_tokens.dtype),
        in_specs=[
            pl.BlockSpec(memory_space=pltpu.VMEM),
            pl.BlockSpec(memory_space=pltpu.VMEM),
        ],
        out_specs=pl.BlockSpec(memory_space=pltpu.VMEM),
    )(select, step_tokens)


def route_tables(step_ids, step_weights, experts, capacity):
    row_count, top_count = step_ids.shape
    pair_count = row_count * top_count
    flat_ids = step_ids.reshape(pair_count)
    onehot = (flat_ids[:, None] == jnp.arange(experts, dtype=jnp.int32)[None, :]).astype(
        jnp.float32
    )
    earlier = (jnp.arange(pair_count)[:, None] > jnp.arange(pair_count)[None, :]).astype(
        jnp.float32
    )
    counts = jnp.dot(earlier, onehot, precision=lax.Precision.HIGHEST)
    slot_index = jnp.sum(counts * onehot, axis=1).astype(jnp.int32)
    position = flat_ids * capacity + slot_index
    placing = (
        position[:, None] == jnp.arange(experts * capacity, dtype=jnp.int32)[None, :]
    ).astype(jnp.float32)
    owner = (
        (jnp.arange(pair_count) // top_count)[:, None] == jnp.arange(row_count)[None, :]
    ).astype(jnp.float32)
    dispatch = jnp.dot(placing.T, owner, precision=lax.Precision.HIGHEST).astype(jnp.bfloat16)
    combine = jnp.dot(
        (owner * step_weights.reshape(pair_count)[:, None]).T,
        placing,
        precision=lax.Precision.HIGHEST,
    )
    return (dispatch, combine)


def join_halves(mine, partner, upper_side, axis_no):
    return jnp.where(
        upper_side,
        jnp.concatenate([partner, mine], axis=axis_no),
        jnp.concatenate([mine, partner], axis=axis_no),
    )


def shared_expert(tokens, shared_weights):
    my_index = lax.axis_index("ep")
    step_count, row_count, model_width = tokens.shape
    gathered = tokens
    for level in (2, 1, 0):
        partner = partner_2(gathered, "ep", level)
        gathered = join_halves(gathered, partner, my_index >> level & 1 == 1, 1)
    flat_rows = gathered.reshape(-1, model_width)
    gate_val = jnp.dot(flat_rows, shared_weights[0], preferred_element_type=jnp.float32)
    up_val = jnp.dot(flat_rows, shared_weights[1], preferred_element_type=jnp.float32)
    hidden = (jax.nn.silu(gate_val) * up_val).astype(jnp.bfloat16)
    partial_value = lax.dot_general(
        hidden, shared_weights[2], (((1,), (1,)), ((), ())), preferred_element_type=jnp.float32
    )
    partial_value = partial_value.reshape(step_count, 8 * row_count, model_width)
    for level in (0, 1, 2):
        half = partial_value.shape[1] // 2
        bit = my_index >> level & 1
        keep = lax.dynamic_slice_in_dim(partial_value, bit * half, half, 1)
        send = lax.dynamic_slice_in_dim(partial_value, (1 - bit) * half, half, 1)
        partial_value = keep + partner_2(send, "ep", level)
    return partial_value


def shards(tokens, expert_ids, combine_weights, w_gate, w_up, w_down, shared_weights):
    step_count, row_count, model_width = tokens.shape
    top_count = expert_ids.shape[2]
    device_count = lax.axis_size("ep")
    experts = w_gate.shape[0] * device_count
    capacity = max(2, row_count * top_count * 2 // experts)
    routed_steps = []
    for s in range(step_count):
        dispatch, combine = route_tables(expert_ids[s], combine_weights[s], experts, capacity)
        outgoing = dispatch_rows(dispatch, tokens[s], experts, capacity)
        received = lax.all_to_all(outgoing, "ep", split_axis=0, concat_axis=0, tiled=True)
        expert_out = expert_rows(received, w_gate, w_up, w_down)
        returned = lax.all_to_all(expert_out, "ep", split_axis=0, concat_axis=0, tiled=True)
        routed_steps.append(
            jnp.einsum(
                "tec,ecd->td",
                combine.reshape(row_count, experts, capacity),
                returned.astype(jnp.float32),
                precision=lax.Precision.HIGHEST,
            )
        )
    shared = shared_expert(tokens, shared_weights)
    routed = jnp.stack(routed_steps)
    return (shared + routed).astype(jnp.bfloat16)


def solution(mesh):
    placed = (
        P(None, "ep", None),
        P(None, "ep", None),
        P(None, "ep", None),
        P("ep", None, None),
        P("ep", None, None),
        P("ep", None, None),
        P(None, None, "ep"),
    )
    return jax.shard_map(
        shards, mesh=mesh, in_specs=placed, out_specs=P(None, "ep", None), check_vma=False
    )
```

```python
import jax
import jax.numpy as jnp
from jax import lax
from jax.sharding import PartitionSpec as P
from jax.experimental import pallas as pl
from jax.experimental.pallas import tpu as pltpu


def partner_2(block, axis, apart):
    count = lax.axis_size(axis)
    route = []
    for low in range(count):
        high = low | 1 << apart
        if high != low and high < count:
            route += [(low, high), (high, low)]
    return lax.ppermute(block, axis, route)


def ffn_kernel(x_ref, gate_ref, up_ref, down_ref, out_ref, total):
    step = pl.program_id(0)

    @pl.when(step == 0)
    def _():
        total[...] = jnp.zeros_like(total)

    rows = x_ref[...].reshape(-1, x_ref.shape[-1])
    gate_val = jnp.dot(rows, gate_ref[...], preferred_element_type=jnp.float32)
    up_val = jnp.dot(rows, up_ref[...], preferred_element_type=jnp.float32)
    hidden = (gate_val / (1.0 + jnp.exp(-gate_val)) * up_val).astype(jnp.bfloat16)
    total[...] += jnp.dot(hidden, down_ref[...], preferred_element_type=jnp.float32)

    @pl.when(step == pl.num_programs(0) - 1)
    def _():
        out_ref[...] = total[...].astype(out_ref.dtype).reshape(out_ref.shape)


def expert_rows(token_block, w_gate, w_up, w_down, tile=256):
    model_width = token_block.shape[-1]
    row_count = token_block.size // model_width
    hidden_width = w_gate.shape[2]
    steps = hidden_width // tile
    flops = 6 * row_count * model_width * hidden_width
    weight_bytes = 3 * model_width * hidden_width * 2
    whole = (0,) * token_block.ndim
    return pl.pallas_call(
        ffn_kernel,
        out_shape=jax.ShapeDtypeStruct(token_block.shape, jnp.bfloat16),
        grid=(steps,),
        in_specs=[
            pl.BlockSpec(token_block.shape, lambda f: whole),
            pl.BlockSpec((None, model_width, tile), lambda f: (0, 0, f)),
            pl.BlockSpec((None, model_width, tile), lambda f: (0, 0, f)),
            pl.BlockSpec((None, tile, model_width), lambda f: (0, f, 0)),
        ],
        out_specs=pl.BlockSpec(token_block.shape, lambda f: whole),
        scratch_shapes=[pltpu.VMEM((row_count, model_width), jnp.float32)],
        compiler_params=pltpu.CompilerParams(
            dimension_semantics=("arbitrary",), vmem_limit_bytes=60 * 1024 * 1024
        ),
        cost_estimate=pl.CostEstimate(
            flops=flops,
            transcendentals=row_count * hidden_width,
            bytes_accessed=weight_bytes + 4 * row_count * model_width,
        ),
    )(token_block, w_gate, w_up, w_down)


def dispatch_kernel(select_ref, token_ref, out_ref):
    picked = jnp.dot(select_ref[...], token_ref[...], preferred_element_type=jnp.float32)
    out_ref[...] = picked.astype(out_ref.dtype).reshape(out_ref.shape)


def dispatch_rows(select, step_tokens, experts, capacity):
    model_width = step_tokens.shape[-1]
    return pl.pallas_call(
        dispatch_kernel,
        out_shape=jax.ShapeDtypeStruct((experts, capacity, model_width), step_tokens.dtype),
        in_specs=[
            pl.BlockSpec(memory_space=pltpu.VMEM),
            pl.BlockSpec(memory_space=pltpu.VMEM),
        ],
        out_specs=pl.BlockSpec(memory_space=pltpu.VMEM),
    )(select, step_tokens)


def route_tables(step_ids, step_weights, experts, capacity):
    row_count, top_count = step_ids.shape
    pair_count = row_count * top_count
    flat_ids = step_ids.reshape(pair_count)
    onehot = (flat_ids[:, None] == jnp.arange(experts, dtype=jnp.int32)[None, :]).astype(
        jnp.float32
    )
    earlier = (jnp.arange(pair_count)[:, None] > jnp.arange(pair_count)[None, :]).astype(
        jnp.float32
    )
    counts = jnp.dot(earlier, onehot, precision=lax.Precision.HIGHEST)
    slot_index = jnp.sum(counts * onehot, axis=1).astype(jnp.int32)
    position = flat_ids * capacity + slot_index
    placing = (
        position[:, None] == jnp.arange(experts * capacity, dtype=jnp.int32)[None, :]
    ).astype(jnp.float32)
    owner = (
        (jnp.arange(pair_count) // top_count)[:, None] == jnp.arange(row_count)[None, :]
    ).astype(jnp.float32)
    dispatch = jnp.dot(placing.T, owner, precision=lax.Precision.HIGHEST).astype(jnp.bfloat16)
    combine = jnp.dot(
        (owner * step_weights.reshape(pair_count)[:, None]).T,
        placing,
        precision=lax.Precision.HIGHEST,
    )
    return (dispatch, combine)


def join_halves(mine, partner, upper_side, axis_no):
    return jnp.where(
        upper_side,
        jnp.concatenate([partner, mine], axis=axis_no),
        jnp.concatenate([mine, partner], axis=axis_no),
    )


def xor_partner(block, mask):
    count = lax.axis_size("ep")
    return lax.ppermute(block, "ep", [(low, low ^ mask) for low in range(count)])


def shared_expert(tokens, shared_weights, group=8):
    step_count, row_count, model_width = tokens.shape
    pieces = [tokens] + [xor_partner(tokens, mask) for mask in range(1, group)]
    gathered = jnp.concatenate(pieces, axis=1)
    flat_rows = gathered.reshape(-1, model_width)
    gate_val = jnp.dot(flat_rows, shared_weights[0], preferred_element_type=jnp.float32)
    up_val = jnp.dot(flat_rows, shared_weights[1], preferred_element_type=jnp.float32)
    hidden = (jax.nn.silu(gate_val) * up_val).astype(jnp.bfloat16)
    partial_value = lax.dot_general(
        hidden, shared_weights[2], (((1,), (1,)), ((), ())), preferred_element_type=jnp.float32
    )
    partial_value = partial_value.reshape(step_count, group, row_count, model_width)
    level = 0
    while partial_value.shape[1] > 1:
        keep = partial_value[:, 0::2]
        send = partial_value[:, 1::2]
        partial_value = keep + xor_partner(send, 1 << level)
        level += 1
    return partial_value[:, 0]


def shards(tokens, expert_ids, combine_weights, w_gate, w_up, w_down, shared_weights):
    step_count, row_count, model_width = tokens.shape
    top_count = expert_ids.shape[2]
    device_count = lax.axis_size("ep")
    experts = w_gate.shape[0] * device_count
    capacity = max(2, row_count * top_count * 2 // experts)
    routed_steps = []
    for s in range(step_count):
        dispatch, combine = route_tables(expert_ids[s], combine_weights[s], experts, capacity)
        outgoing = dispatch_rows(dispatch, tokens[s], experts, capacity)
        received = lax.all_to_all(outgoing, "ep", split_axis=0, concat_axis=0, tiled=True)
        expert_out = expert_rows(received, w_gate, w_up, w_down)
        returned = lax.all_to_all(expert_out, "ep", split_axis=0, concat_axis=0, tiled=True)
        routed_steps.append(
            jnp.einsum(
                "tec,ecd->td",
                combine.reshape(row_count, experts, capacity),
                returned.astype(jnp.float32),
                precision=lax.Precision.HIGHEST,
            )
        )
    shared = shared_expert(tokens, shared_weights)
    routed = jnp.stack(routed_steps)
    return (shared + routed).astype(jnp.bfloat16)


def solution(mesh):
    placed = (
        P(None, "ep", None),
        P(None, "ep", None),
        P(None, "ep", None),
        P("ep", None, None),
        P("ep", None, None),
        P("ep", None, None),
        P(None, None, "ep"),
    )
    return jax.shard_map(
        shards, mesh=mesh, in_specs=placed, out_specs=P(None, "ep", None), check_vma=False
    )
```

```python
import jax
import jax.numpy as jnp
from jax import lax
from jax.sharding import PartitionSpec as P
from jax.experimental import pallas as pl
from jax.experimental.pallas import tpu as pltpu


def partner_2(block, axis, apart):
    count = lax.axis_size(axis)
    route = []
    for low in range(count):
        high = low | 1 << apart
        if high != low and high < count:
            route += [(low, high), (high, low)]
    return lax.ppermute(block, axis, route)


def ffn_kernel(x_ref, gate_ref, up_ref, down_ref, out_ref, total):
    step = pl.program_id(0)

    @pl.when(step == 0)
    def _():
        total[...] = jnp.zeros_like(total)

    rows = x_ref[...].reshape(-1, x_ref.shape[-1])
    gate_val = jnp.dot(rows, gate_ref[...], preferred_element_type=jnp.float32)
    up_val = jnp.dot(rows, up_ref[...], preferred_element_type=jnp.float32)
    hidden = (gate_val / (1.0 + jnp.exp(-gate_val)) * up_val).astype(jnp.bfloat16)
    total[...] += jnp.dot(hidden, down_ref[...], preferred_element_type=jnp.float32)

    @pl.when(step == pl.num_programs(0) - 1)
    def _():
        out_ref[...] = total[...].astype(out_ref.dtype).reshape(out_ref.shape)


def expert_rows(token_block, w_gate, w_up, w_down, tile=256):
    model_width = token_block.shape[-1]
    row_count = token_block.size // model_width
    hidden_width = w_gate.shape[2]
    steps = hidden_width // tile
    flops = 6 * row_count * model_width * hidden_width
    weight_bytes = 3 * model_width * hidden_width * 2
    whole = (0,) * token_block.ndim
    return pl.pallas_call(
        ffn_kernel,
        out_shape=jax.ShapeDtypeStruct(token_block.shape, jnp.bfloat16),
        grid=(steps,),
        in_specs=[
            pl.BlockSpec(token_block.shape, lambda f: whole),
            pl.BlockSpec((None, model_width, tile), lambda f: (0, 0, f)),
            pl.BlockSpec((None, model_width, tile), lambda f: (0, 0, f)),
            pl.BlockSpec((None, tile, model_width), lambda f: (0, f, 0)),
        ],
        out_specs=pl.BlockSpec(token_block.shape, lambda f: whole),
        scratch_shapes=[pltpu.VMEM((row_count, model_width), jnp.float32)],
        compiler_params=pltpu.CompilerParams(
            dimension_semantics=("arbitrary",), vmem_limit_bytes=60 * 1024 * 1024
        ),
        cost_estimate=pl.CostEstimate(
            flops=flops,
            transcendentals=row_count * hidden_width,
            bytes_accessed=weight_bytes + 4 * row_count * model_width,
        ),
    )(token_block, w_gate, w_up, w_down)


def dispatch_kernel(select_ref, token_ref, out_ref):
    picked = jnp.dot(select_ref[...], token_ref[...], preferred_element_type=jnp.float32)
    out_ref[...] = picked.astype(out_ref.dtype).reshape(out_ref.shape)


def dispatch_rows(select, step_tokens, experts, capacity):
    model_width = step_tokens.shape[-1]
    return pl.pallas_call(
        dispatch_kernel,
        out_shape=jax.ShapeDtypeStruct((experts, capacity, model_width), step_tokens.dtype),
        in_specs=[
            pl.BlockSpec(memory_space=pltpu.VMEM),
            pl.BlockSpec(memory_space=pltpu.VMEM),
        ],
        out_specs=pl.BlockSpec(memory_space=pltpu.VMEM),
    )(select, step_tokens)


def route_tables(step_ids, step_weights, experts, capacity):
    row_count, top_count = step_ids.shape
    pair_count = row_count * top_count
    flat_ids = step_ids.reshape(pair_count)
    onehot = (flat_ids[:, None] == jnp.arange(experts, dtype=jnp.int32)[None, :]).astype(
        jnp.float32
    )
    earlier = (jnp.arange(pair_count)[:, None] > jnp.arange(pair_count)[None, :]).astype(
        jnp.float32
    )
    counts = jnp.dot(earlier, onehot, precision=lax.Precision.HIGHEST)
    slot_index = jnp.sum(counts * onehot, axis=1).astype(jnp.int32)
    position = flat_ids * capacity + slot_index
    placing = (
        position[:, None] == jnp.arange(experts * capacity, dtype=jnp.int32)[None, :]
    ).astype(jnp.float32)
    owner = (
        (jnp.arange(pair_count) // top_count)[:, None] == jnp.arange(row_count)[None, :]
    ).astype(jnp.float32)
    dispatch = jnp.dot(placing.T, owner, precision=lax.Precision.HIGHEST).astype(jnp.bfloat16)
    combine = jnp.dot(
        (owner * step_weights.reshape(pair_count)[:, None]).T,
        placing,
        precision=lax.Precision.HIGHEST,
    )
    return (dispatch, combine)


def join_halves(mine, partner, upper_side, axis_no):
    return jnp.where(
        upper_side,
        jnp.concatenate([partner, mine], axis=axis_no),
        jnp.concatenate([mine, partner], axis=axis_no),
    )


def gray_partner(low, mask):
    base, rank = low - low % 8, low % 8
    place = rank >> 1
    label = (place ^ place >> 1) << 1 | rank & 1
    label ^= mask
    code = label >> 1
    return base + (code ^ code >> 1) * 2 + (label & 1)


def xor_partner(block, mask):
    count = lax.axis_size("ep")
    return lax.ppermute(block, "ep", [(low, gray_partner(low, mask)) for low in range(count)])


def shared_expert(tokens, shared_weights, group=8):
    step_count, row_count, model_width = tokens.shape
    pieces = [tokens] + [xor_partner(tokens, mask) for mask in range(1, group)]
    gathered = jnp.concatenate(pieces, axis=1)
    flat_rows = gathered.reshape(-1, model_width)
    gate_val = jnp.dot(flat_rows, shared_weights[0], preferred_element_type=jnp.float32)
    up_val = jnp.dot(flat_rows, shared_weights[1], preferred_element_type=jnp.float32)
    hidden = (jax.nn.silu(gate_val) * up_val).astype(jnp.bfloat16)
    partial_value = lax.dot_general(
        hidden, shared_weights[2], (((1,), (1,)), ((), ())), preferred_element_type=jnp.float32
    )
    partial_value = partial_value.reshape(step_count, group, row_count, model_width)
    level = 0
    while partial_value.shape[1] > 1:
        keep = partial_value[:, 0::2]
        send = partial_value[:, 1::2]
        partial_value = keep + xor_partner(send, 1 << level)
        level += 1
    return partial_value[:, 0]


def shards(tokens, expert_ids, combine_weights, w_gate, w_up, w_down, shared_weights):
    step_count, row_count, model_width = tokens.shape
    top_count = expert_ids.shape[2]
    device_count = lax.axis_size("ep")
    experts = w_gate.shape[0] * device_count
    capacity = max(2, row_count * top_count * 2 // experts)
    routed_steps = []
    for s in range(step_count):
        dispatch, combine = route_tables(expert_ids[s], combine_weights[s], experts, capacity)
        outgoing = dispatch_rows(dispatch, tokens[s], experts, capacity)
        received = lax.all_to_all(outgoing, "ep", split_axis=0, concat_axis=0, tiled=True)
        expert_out = expert_rows(received, w_gate, w_up, w_down)
        returned = lax.all_to_all(expert_out, "ep", split_axis=0, concat_axis=0, tiled=True)
        routed_steps.append(
            jnp.einsum(
                "tec,ecd->td",
                combine.reshape(row_count, experts, capacity),
                returned.astype(jnp.float32),
                precision=lax.Precision.HIGHEST,
            )
        )
    shared = shared_expert(tokens, shared_weights)
    routed = jnp.stack(routed_steps)
    return (shared + routed).astype(jnp.bfloat16)


def solution(mesh):
    placed = (
        P(None, "ep", None),
        P(None, "ep", None),
        P(None, "ep", None),
        P("ep", None, None),
        P("ep", None, None),
        P("ep", None, None),
        P(None, None, "ep"),
    )
    return jax.shard_map(
        shards, mesh=mesh, in_specs=placed, out_specs=P(None, "ep", None), check_vma=False
    )
```

```python
import jax
import jax.numpy as jnp
from jax import lax
from jax.sharding import PartitionSpec as P
from jax.experimental import pallas as pl
from jax.experimental.pallas import tpu as pltpu


def partner_2(block, axis, apart):
    count = lax.axis_size(axis)
    route = []
    for low in range(count):
        high = low | 1 << apart
        if high != low and high < count:
            route += [(low, high), (high, low)]
    return lax.ppermute(block, axis, route)


def ffn_kernel(x_ref, gate_ref, up_ref, down_ref, out_ref, total):
    step = pl.program_id(0)

    @pl.when(step == 0)
    def _():
        total[...] = jnp.zeros_like(total)

    rows = x_ref[...].reshape(-1, x_ref.shape[-1])
    gate_val = jnp.dot(rows, gate_ref[...], preferred_element_type=jnp.float32)
    up_val = jnp.dot(rows, up_ref[...], preferred_element_type=jnp.float32)
    hidden = (gate_val / (1.0 + jnp.exp(-gate_val)) * up_val).astype(jnp.bfloat16)
    total[...] += jnp.dot(hidden, down_ref[...], preferred_element_type=jnp.float32)

    @pl.when(step == pl.num_programs(0) - 1)
    def _():
        out_ref[...] = total[...].astype(out_ref.dtype).reshape(out_ref.shape)


def expert_rows(token_block, w_gate, w_up, w_down, tile=256):
    model_width = token_block.shape[-1]
    row_count = token_block.size // model_width
    hidden_width = w_gate.shape[2]
    steps = hidden_width // tile
    flops = 6 * row_count * model_width * hidden_width
    weight_bytes = 3 * model_width * hidden_width * 2
    whole = (0,) * token_block.ndim
    return pl.pallas_call(
        ffn_kernel,
        out_shape=jax.ShapeDtypeStruct(token_block.shape, jnp.bfloat16),
        grid=(steps,),
        in_specs=[
            pl.BlockSpec(token_block.shape, lambda f: whole),
            pl.BlockSpec((None, model_width, tile), lambda f: (0, 0, f)),
            pl.BlockSpec((None, model_width, tile), lambda f: (0, 0, f)),
            pl.BlockSpec((None, tile, model_width), lambda f: (0, f, 0)),
        ],
        out_specs=pl.BlockSpec(token_block.shape, lambda f: whole),
        scratch_shapes=[pltpu.VMEM((row_count, model_width), jnp.float32)],
        compiler_params=pltpu.CompilerParams(
            dimension_semantics=("arbitrary",), vmem_limit_bytes=60 * 1024 * 1024
        ),
        cost_estimate=pl.CostEstimate(
            flops=flops,
            transcendentals=row_count * hidden_width,
            bytes_accessed=weight_bytes + 4 * row_count * model_width,
        ),
    )(token_block, w_gate, w_up, w_down)


def dispatch_kernel(select_ref, token_ref, out_ref):
    picked = jnp.dot(select_ref[...], token_ref[...], preferred_element_type=jnp.float32)
    out_ref[...] = picked.astype(out_ref.dtype).reshape(out_ref.shape)


def dispatch_rows(select, step_tokens, experts, capacity):
    model_width = step_tokens.shape[-1]
    return pl.pallas_call(
        dispatch_kernel,
        out_shape=jax.ShapeDtypeStruct((experts, capacity, model_width), step_tokens.dtype),
        in_specs=[
            pl.BlockSpec(memory_space=pltpu.VMEM),
            pl.BlockSpec(memory_space=pltpu.VMEM),
        ],
        out_specs=pl.BlockSpec(memory_space=pltpu.VMEM),
    )(select, step_tokens)


def route_tables(step_ids, step_weights, experts, capacity):
    row_count, top_count = step_ids.shape
    pair_count = row_count * top_count
    flat_ids = step_ids.reshape(pair_count)
    onehot = (flat_ids[:, None] == jnp.arange(experts, dtype=jnp.int32)[None, :]).astype(
        jnp.float32
    )
    earlier = (jnp.arange(pair_count)[:, None] > jnp.arange(pair_count)[None, :]).astype(
        jnp.float32
    )
    counts = jnp.dot(earlier, onehot, precision=lax.Precision.HIGHEST)
    slot_index = jnp.sum(counts * onehot, axis=1).astype(jnp.int32)
    position = flat_ids * capacity + slot_index
    placing = (
        position[:, None] == jnp.arange(experts * capacity, dtype=jnp.int32)[None, :]
    ).astype(jnp.float32)
    owner = (
        (jnp.arange(pair_count) // top_count)[:, None] == jnp.arange(row_count)[None, :]
    ).astype(jnp.float32)
    dispatch = jnp.dot(placing.T, owner, precision=lax.Precision.HIGHEST).astype(jnp.bfloat16)
    combine = jnp.dot(
        (owner * step_weights.reshape(pair_count)[:, None]).T,
        placing,
        precision=lax.Precision.HIGHEST,
    )
    return (dispatch, combine)


def join_halves(mine, partner, upper_side, axis_no):
    return jnp.where(
        upper_side,
        jnp.concatenate([partner, mine], axis=axis_no),
        jnp.concatenate([mine, partner], axis=axis_no),
    )


def gray_partner(low, mask):
    base, rank = low - low % 8, low % 8
    place = rank >> 1
    label = (place ^ place >> 1) << 1 | rank & 1
    label ^= mask
    code = label >> 1
    return base + (code ^ code >> 1) * 2 + (label & 1)


def xor_partner(block, mask):
    count = lax.axis_size("ep")
    return lax.ppermute(block, "ep", [(low, gray_partner(low, mask)) for low in range(count)])


def shared_expert(tokens, shared_weights, group=8):
    step_count, row_count, model_width = tokens.shape
    pieces = [tokens] + [xor_partner(tokens, mask) for mask in range(1, group)]
    gathered = jnp.concatenate(pieces, axis=1)
    flat_rows = gathered.reshape(-1, model_width)
    gate_val = jnp.dot(flat_rows, shared_weights[0], preferred_element_type=jnp.float32)
    up_val = jnp.dot(flat_rows, shared_weights[1], preferred_element_type=jnp.float32)
    hidden = (jax.nn.silu(gate_val) * up_val).astype(jnp.bfloat16)
    partial_value = lax.dot_general(
        hidden, shared_weights[2], (((1,), (1,)), ((), ())), preferred_element_type=jnp.float32
    )
    partial_value = partial_value.reshape(step_count, group, row_count, model_width)
    partial_value = partial_value[:, 0::2] + xor_partner(partial_value[:, 1::2], 1)
    total = partial_value[:, 0]
    for slot in range(1, group // 2):
        total = total + xor_partner(partial_value[:, slot], slot * 2)
    return total


def shards(tokens, expert_ids, combine_weights, w_gate, w_up, w_down, shared_weights):
    step_count, row_count, model_width = tokens.shape
    top_count = expert_ids.shape[2]
    device_count = lax.axis_size("ep")
    experts = w_gate.shape[0] * device_count
    capacity = max(2, row_count * top_count * 2 // experts)
    routed_steps = []
    for s in range(step_count):
        dispatch, combine = route_tables(expert_ids[s], combine_weights[s], experts, capacity)
        outgoing = dispatch_rows(dispatch, tokens[s], experts, capacity)
        received = lax.all_to_all(outgoing, "ep", split_axis=0, concat_axis=0, tiled=True)
        expert_out = expert_rows(received, w_gate, w_up, w_down)
        returned = lax.all_to_all(expert_out, "ep", split_axis=0, concat_axis=0, tiled=True)
        routed_steps.append(
            jnp.einsum(
                "tec,ecd->td",
                combine.reshape(row_count, experts, capacity),
                returned.astype(jnp.float32),
                precision=lax.Precision.HIGHEST,
            )
        )
    shared = shared_expert(tokens, shared_weights)
    routed = jnp.stack(routed_steps)
    return (shared + routed).astype(jnp.bfloat16)


def solution(mesh):
    placed = (
        P(None, "ep", None),
        P(None, "ep", None),
        P(None, "ep", None),
        P("ep", None, None),
        P("ep", None, None),
        P("ep", None, None),
        P(None, None, "ep"),
    )
    return jax.shard_map(
        shards, mesh=mesh, in_specs=placed, out_specs=P(None, "ep", None), check_vma=False
    )
```

```python
import jax
import jax.numpy as jnp
from jax import lax
from jax.sharding import PartitionSpec as P
from jax.experimental import pallas as pl
from jax.experimental.pallas import tpu as pltpu


def partner_2(block, axis, apart):
    count = lax.axis_size(axis)
    route = []
    for low in range(count):
        high = low | 1 << apart
        if high != low and high < count:
            route += [(low, high), (high, low)]
    return lax.ppermute(block, axis, route)


def ffn_kernel(x_ref, gate_ref, up_ref, down_ref, out_ref, total):
    step = pl.program_id(0)

    @pl.when(step == 0)
    def _():
        total[...] = jnp.zeros_like(total)

    rows = x_ref[...].reshape(-1, x_ref.shape[-1])
    gate_val = jnp.dot(rows, gate_ref[...], preferred_element_type=jnp.float32)
    up_val = jnp.dot(rows, up_ref[...], preferred_element_type=jnp.float32)
    hidden = (gate_val / (1.0 + jnp.exp(-gate_val)) * up_val).astype(jnp.bfloat16)
    total[...] += jnp.dot(hidden, down_ref[...], preferred_element_type=jnp.float32)

    @pl.when(step == pl.num_programs(0) - 1)
    def _():
        out_ref[...] = total[...].astype(out_ref.dtype).reshape(out_ref.shape)


def expert_rows(token_block, w_gate, w_up, w_down, tile=256):
    model_width = token_block.shape[-1]
    row_count = token_block.size // model_width
    hidden_width = w_gate.shape[2]
    steps = hidden_width // tile
    flops = 6 * row_count * model_width * hidden_width
    weight_bytes = 3 * model_width * hidden_width * 2
    whole = (0,) * token_block.ndim
    return pl.pallas_call(
        ffn_kernel,
        out_shape=jax.ShapeDtypeStruct(token_block.shape, jnp.bfloat16),
        grid=(steps,),
        in_specs=[
            pl.BlockSpec(token_block.shape, lambda f: whole),
            pl.BlockSpec((None, model_width, tile), lambda f: (0, 0, f)),
            pl.BlockSpec((None, model_width, tile), lambda f: (0, 0, f)),
            pl.BlockSpec((None, tile, model_width), lambda f: (0, f, 0)),
        ],
        out_specs=pl.BlockSpec(token_block.shape, lambda f: whole),
        scratch_shapes=[pltpu.VMEM((row_count, model_width), jnp.float32)],
        compiler_params=pltpu.CompilerParams(
            dimension_semantics=("arbitrary",), vmem_limit_bytes=60 * 1024 * 1024
        ),
        cost_estimate=pl.CostEstimate(
            flops=flops,
            transcendentals=row_count * hidden_width,
            bytes_accessed=weight_bytes + 4 * row_count * model_width,
        ),
    )(token_block, w_gate, w_up, w_down)


def dispatch_kernel(select_ref, token_ref, out_ref):
    picked = jnp.dot(select_ref[...], token_ref[...], preferred_element_type=jnp.float32)
    out_ref[...] = picked.astype(out_ref.dtype).reshape(out_ref.shape)


def dispatch_rows(select, step_tokens, experts, capacity):
    model_width = step_tokens.shape[-1]
    return pl.pallas_call(
        dispatch_kernel,
        out_shape=jax.ShapeDtypeStruct((experts, capacity, model_width), step_tokens.dtype),
        in_specs=[
            pl.BlockSpec(memory_space=pltpu.VMEM),
            pl.BlockSpec(memory_space=pltpu.VMEM),
        ],
        out_specs=pl.BlockSpec(memory_space=pltpu.VMEM),
    )(select, step_tokens)


def route_tables(step_ids, step_weights, experts, capacity):
    row_count, top_count = step_ids.shape
    pair_count = row_count * top_count
    flat_ids = step_ids.reshape(pair_count)
    onehot = (flat_ids[:, None] == jnp.arange(experts, dtype=jnp.int32)[None, :]).astype(
        jnp.float32
    )
    earlier = (jnp.arange(pair_count)[:, None] > jnp.arange(pair_count)[None, :]).astype(
        jnp.float32
    )
    counts = jnp.dot(earlier, onehot, precision=lax.Precision.HIGHEST)
    slot_index = jnp.sum(counts * onehot, axis=1).astype(jnp.int32)
    position = flat_ids * capacity + slot_index
    placing = (
        position[:, None] == jnp.arange(experts * capacity, dtype=jnp.int32)[None, :]
    ).astype(jnp.float32)
    owner = (
        (jnp.arange(pair_count) // top_count)[:, None] == jnp.arange(row_count)[None, :]
    ).astype(jnp.float32)
    dispatch = jnp.dot(placing.T, owner, precision=lax.Precision.HIGHEST).astype(jnp.bfloat16)
    combine = jnp.dot(
        (owner * step_weights.reshape(pair_count)[:, None]).T,
        placing,
        precision=lax.Precision.HIGHEST,
    )
    return (dispatch, combine)


def join_halves(mine, partner, upper_side, axis_no):
    return jnp.where(
        upper_side,
        jnp.concatenate([partner, mine], axis=axis_no),
        jnp.concatenate([mine, partner], axis=axis_no),
    )


def gray_partner(low, mask):
    base, rank = low - low % 8, low % 8
    place = rank >> 1
    label = (place ^ place >> 1) << 1 | rank & 1
    label ^= mask
    code = label >> 1
    return base + (code ^ code >> 1) * 2 + (label & 1)


def xor_partner(block, mask):
    count = lax.axis_size("ep")
    return lax.ppermute(block, "ep", [(low, gray_partner(low, mask)) for low in range(count)])


def shared_partials(tokens, shared_weights, group=8):
    step_count, row_count, model_width = tokens.shape
    pieces = [tokens] + [xor_partner(tokens, mask) for mask in range(1, group)]
    gathered = jnp.concatenate(pieces, axis=1)
    flat_rows = gathered.reshape(-1, model_width)
    gate_val = jnp.dot(flat_rows, shared_weights[0], preferred_element_type=jnp.float32)
    up_val = jnp.dot(flat_rows, shared_weights[1], preferred_element_type=jnp.float32)
    hidden = (jax.nn.silu(gate_val) * up_val).astype(jnp.bfloat16)
    partial_value = lax.dot_general(
        hidden, shared_weights[2], (((1,), (1,)), ((), ())), preferred_element_type=jnp.float32
    )
    partial_value = partial_value.reshape(step_count, group, row_count, model_width)
    return partial_value[:, 0::2] + xor_partner(partial_value[:, 1::2], 1)


def shared_finish(partial_value, group=8):
    total = partial_value[:, 0]
    for slot in range(1, group // 2):
        total = total + xor_partner(partial_value[:, slot], slot * 2)
    return total


def shards(tokens, expert_ids, combine_weights, w_gate, w_up, w_down, shared_weights):
    step_count, row_count, model_width = tokens.shape
    top_count = expert_ids.shape[2]
    device_count = lax.axis_size("ep")
    experts = w_gate.shape[0] * device_count
    capacity = max(2, row_count * top_count * 2 // experts)
    chip_sums = shared_partials(tokens, shared_weights)
    routed_steps = []
    for s in range(step_count):
        dispatch, combine = route_tables(expert_ids[s], combine_weights[s], experts, capacity)
        outgoing = dispatch_rows(dispatch, tokens[s], experts, capacity)
        received = lax.all_to_all(outgoing, "ep", split_axis=0, concat_axis=0, tiled=True)
        if s == step_count - 1:
            received, chip_sums = lax.optimization_barrier((received, chip_sums))
        expert_out = expert_rows(received, w_gate, w_up, w_down)
        returned = lax.all_to_all(expert_out, "ep", split_axis=0, concat_axis=0, tiled=True)
        routed_steps.append(
            jnp.einsum(
                "tec,ecd->td",
                combine.reshape(row_count, experts, capacity),
                returned.astype(jnp.float32),
                precision=lax.Precision.HIGHEST,
            )
        )
    shared = shared_finish(chip_sums)
    routed = jnp.stack(routed_steps)
    return (shared + routed).astype(jnp.bfloat16)


def solution(mesh):
    placed = (
        P(None, "ep", None),
        P(None, "ep", None),
        P(None, "ep", None),
        P("ep", None, None),
        P("ep", None, None),
        P("ep", None, None),
        P(None, None, "ep"),
    )
    return jax.shard_map(
        shards, mesh=mesh, in_specs=placed, out_specs=P(None, "ep", None), check_vma=False
    )
```
